32 devices in a mesh: sec: 2 (over y), dev: 16 (over z, x, core).
Axes of the slice: x: 2, y: 2, z: 4, core: 2. Of those that a mesh axis runs over, the one named last changes fastest.
Arguments:
- flow_state: float32 [5, 8, 1024, 512], P(None, None, ('sec', 'dev')), may hold values from -6 to 6
- diffusion: float32 [8, 1024, 512], P(None, ('sec', 'dev')), may hold values from 0.02 to 0.1
- wall_stress: float32 [2, 1024, 512], P(None, ('sec', 'dev')), may hold values from -3 to 3
- batch_counts: int32 [32, 48], P(('sec', 'dev')), may hold values from 1 to 4, 120 in all within a row
- batch_routes: int32 [1536, 1], P(('sec', 'dev')), may hold values from 0 to 31; in each aligned block of 48 rows (0 to 47, 48 to 95, ...) at most 2 rows name the same one
- wall_index: int32 [1536, 4], P(('sec', 'dev')), may hold values from 0 to 16383, as said below
- input_weight: bfloat16 [12, 2048], replicated, may hold values from -1.75 to 1.75
- middle_weight: bfloat16 [2048, 2048], P(('sec', 'dev')), may hold values from -0.125 to 0.125
- output_weight: bfloat16 [2, 2048], replicated, may hold values from -0.125 to 0.125
Outputs:
- new_field: float32 [5, 8, 1024, 512], P(None, None, ('sec', 'dev'))
- new_stress: float32 [2, 1024, 512], P(None, ('sec', 'dev'))
- batch_loss: float32 [32], P(('sec', 'dev'))
- grad_w_in: float32 [12, 2048], replicated
- grad_w_mid: float32 [2048, 2048], P(('sec', 'dev'))
The draws below stay inside these ranges and needn't reach their ends.
Inputs may be any that keep to these rules, and one draw needn't show every extreme that they name: `batch_routes`: within the 48 rows of one device no trainer is named more than 2 times, and every trainer is named by some row. `batch_counts`: each device's row sums to 120. `wall_index`: all entries of the 48 rows of one device are distinct.
All inputs are finite; a program needn't handle non-finite values.
Results may differ from the reference program's by a relative error of at most 0.00091.
Values may be sent and summed in bfloat16 or wider, within the bound.
No kernel may reach another device: no remote copies, remote signals or barrier semaphores. Data moves between devices by JAX's collectives and lax.ppermute only.
A program may use at most 128 MiB of HBM per device.

```python
import math
import jax
import jax.numpy as jnp
import numpy as np
from jax import lax

NV = 5
NL = 8
NX = 512
ZL = 32
CAP = 4
FEAT = 12
H = 2048
SLOTS = 2
NZ = 1024
TILES_DEV = 48
LIVE_DEV = 120
BATCHES = 1536
SAMPLES = 3840
DEVICES = 32


def draw_wall_index(key, part):
    points = ZL * NX
    owners = BATCHES // TILES_DEV
    keys = jax.random.split(key, owners)

    def one_owner(owner_key):
        order = jax.random.permutation(owner_key, points)
        chosen = order[:TILES_DEV * CAP]
        has_top = jnp.any(chosen == points - 1)
        chosen = chosen.at[0].set(jnp.where(has_top, chosen[0], points - 1))
        return chosen.reshape(TILES_DEV, CAP)
    return jax.vmap(one_owner)(keys).reshape(BATCHES, CAP).astype(jnp.int32)


def block_scale(rng, extent, cuts, smallest, top_value):
    def one(axis_at, parts):
        draws = jax.random.uniform(jax.random.fold_in(jax.random.fold_in(rng, 6), axis_at), (parts,), jnp.float32, smallest / len(cuts), top_value / len(cuts))
        return jnp.repeat(jnp.exp(draws), extent[axis_at] // parts).reshape((-1,) + (1,) * (len(extent) - axis_at - 1))

    level = one(*cuts[0])
    for cut in cuts[1:]:
        level = level * one(*cut)
    return level


def profile(count, total, bound, lean):
    portions = [(1 << 20) // math.isqrt(rank ** lean) + 1 for rank in range(2, count + 1)]
    spare, given = total - bound - (count - 1), [1] * (count - 1)
    while spare > 0:
        movable = [i for i in range(count - 1) if given[i] < bound]
        pool, remaining = sum([portions[i] for i in movable]), spare
        for i in movable:
            more = min(bound - given[i], max(1, remaining * portions[i] // pool), spare)
            given[i] = given[i] + more
            spare = spare - more
    return np.array([bound] + given)


def uneven(rng, count, total, limit, skew):
    if count == 2:
        one = jax.random.randint(rng, (), max(1, total - limit), min(limit, total - 1) + 1)
        return jnp.stack([one, total - one])
    tallies = jnp.asarray(profile(count, total, limit, skew), jnp.int32)
    pairs = (count - 1) // 2
    donor, taker = tallies[1:1 + 2 * pairs:2], tallies[2:2 + 2 * pairs:2]
    room = jnp.minimum(donor - 1, limit - taker)
    moved = jax.random.randint(jax.random.fold_in(rng, 1), (pairs,), 0, 1 << 20) % (room + 1)
    tallies = tallies.at[1:1 + 2 * pairs:2].set(donor - moved).at[2:2 + 2 * pairs:2].set(taker + moved)
    return tallies[jax.random.permutation(jax.random.fold_in(rng, 2), count)]


def assign_block(own_key, own, number, rows, amount, top, limit, lean):
    sequence = jax.random.permutation(own_key, amount)
    crowded, usual = load_shares(amount, rows * top, limit, lean, True), load_shares(amount, rows * top, limit, lean, False)
    places = jnp.arange(amount)

    def named(tallies, rotation):
        used = int((tallies > 0).sum())
        fixed = max(1, used // 4)
        shifted = fixed + (places - fixed + rotation * (used - fixed)) % max(1, amount - fixed)
        return jnp.zeros((amount,), jnp.int32).at[sequence[jnp.where(places < fixed, places, shifted)]].set(jnp.asarray(tallies, jnp.int32))

    tallies = jnp.where(number % 4 == 0, named(crowded, number // 4), named(usual, number - number // 4 - 1))
    mixed = jax.random.permutation(jax.random.fold_in(own, 3), amount)
    source_of, taker = mixed[0:amount // 2 * 2:2], mixed[1:amount // 2 * 2:2]
    room = jnp.minimum(tallies[source_of] - 1, limit - tallies[taker]) // 2
    room = jnp.where((source_of == sequence[0]) | (taker == sequence[0]) | (tallies[taker] == 0), 0, jnp.maximum(room, 0))
    shifted = jax.random.randint(jax.random.fold_in(own, 4), (amount // 2,), 0, 1 << 20) % (room + 1)
    tallies = tallies.at[source_of].add(-shifted).at[taker].add(shifted)
    labels = jnp.searchsorted(jnp.cumsum(tallies), jnp.arange(rows * top), side="right").astype(jnp.int32)
    listing = labels.reshape(top, rows).T
    listing = listing[jax.random.permutation(jax.random.fold_in(own, 1), rows)]
    rotation = jax.random.randint(jax.random.fold_in(own, 2), (rows, 1), 0, top)
    return jnp.take_along_axis(listing, (jnp.arange(top)[None, :] + rotation) % top, axis=1)


def load_shares(number_of, total, bound, slope, full):
    weights = [(1 << 20) // math.isqrt(grade ** slope) + 1 for grade in range(1, number_of + 1)]
    largest = bound if full else min(bound, max(-(-total // number_of), total * weights[0] // sum(weights)))
    least = 1 if total - largest >= number_of - 1 else 0
    given, surplus = [largest] + [least] * (number_of - 1), total - largest - least * (number_of - 1)
    while surplus > 0:
        movable = [i for i in range(1, number_of) if given[i] < largest] or [i for i in range(1, number_of) if given[i] < bound]
        pool, remaining = sum([weights[i] for i in movable]), surplus
        for i in movable:
            more = min(bound - given[i], max(1, remaining * weights[i] // pool), surplus)
            given[i] = given[i] + more
            surplus = surplus - more
    return np.array(given)


def scatter_about(rng, shape, width, limit, cuts=(), kind=jnp.bfloat16):
    gain = block_scale(rng, shape, cuts, -0.22, 0.18) if cuts else 1.0
    drawn = jax.random.normal(rng, shape, jnp.float32) * width * gain
    return jnp.minimum(jnp.maximum(drawn, -limit), limit).astype(kind)


def setup_inputs(seed: int = 0) -> dict:
    arg_keys = jax.random.split(jax.random.key(seed), 10)
    flow_state = scatter_about(arg_keys[0], (NV, NL, NZ, NX), 1.0, 6.0, ((2, 32),), jnp.float32)
    diffusion = jnp.clip(jnp.exp(math.log(0.1) - 1.609438 * jax.random.uniform(arg_keys[1], (NL, NZ, NX), jnp.float32) ** block_scale(arg_keys[1], (NL, NZ, NX), ((1, 32),), -0.2, 0.2)), 0.02, 0.1)
    wall_stress = scatter_about(arg_keys[2], (2, NZ, NX), 0.5, 3.0, ((1, 32),), jnp.float32)
    batch_counts = jax.vmap(lambda own: uneven(own, TILES_DEV, LIVE_DEV, CAP, 2))(jax.random.split(arg_keys[3], DEVICES)).reshape((DEVICES, TILES_DEV)).astype(jnp.int32)
    batch_routes_keys = jax.random.split(jax.random.fold_in(arg_keys[4], 1), BATCHES // TILES_DEV)
    batch_routes_turns = jax.random.permutation(jax.random.fold_in(arg_keys[4], 3), BATCHES // TILES_DEV)
    batch_routes = jax.vmap(lambda own, number: assign_block(jax.random.fold_in(arg_keys[4], 2), own, number, TILES_DEV, DEVICES, 1, SLOTS, 2))(batch_routes_keys, batch_routes_turns).reshape((BATCHES, 1))
    wall_index = draw_wall_index(jax.random.fold_in(arg_keys[9], 71), 0)
    input_weight = scatter_about(arg_keys[6], (FEAT, H), FEAT ** -0.5, 1.75)
    middle_weight = scatter_about(arg_keys[7], (H, H), H ** -0.5, 0.125, ((0, 32),))
    output_weight = scatter_about(arg_keys[8], (2, H), H ** -0.5, 0.125)
    return dict(flow_state=flow_state, diffusion=diffusion, wall_stress=wall_stress, batch_counts=batch_counts, batch_routes=batch_routes, wall_index=wall_index, input_weight=input_weight, middle_weight=middle_weight, output_weight=output_weight)


advect_number = 0.3
wall_gain = 0.5
grad_number = 32.0

def advance(flow_state, diffusion, below_z, above_z):
    below_x = jnp.concatenate([flow_state[..., :1], flow_state[..., :-1]], axis=3)
    above_x = jnp.concatenate([flow_state[..., 1:], flow_state[..., -1:]], axis=3)
    below_y = jnp.concatenate([flow_state[:, :1], flow_state[:, :-1]], axis=1)
    above_y = jnp.concatenate([flow_state[:, 1:], flow_state[:, -1:]], axis=1)
    spread = below_x + above_x + below_y + above_y + below_z + above_z - 6.0 * flow_state
    return flow_state + advect_number * (below_x - flow_state) + diffusion[None] * spread

def wall_columns(flow_state):
    points = flow_state.shape[2] * flow_state.shape[3]
    inputs = flow_state[0:4, 0:3].reshape(12, points)
    targets = jnp.stack([flow_state[1, 4] - flow_state[1, 3], flow_state[3, 4] - flow_state[3, 3]]).reshape(2, points)
    return jnp.concatenate([inputs, targets], axis=0).astype(jnp.bfloat16)

def apply_wall(advanced, new_stress):
    advanced = advanced.at[1, 0].add(-wall_gain * new_stress[0])
    return advanced.at[3, 0].add(-wall_gain * new_stress[1])

def reference(flow_state, diffusion, wall_stress, batch_counts, batch_routes, wall_index, input_weight, middle_weight, output_weight):
    owners, tile_count = batch_counts.shape
    batches, capacity = wall_index.shape
    points = ZL * NX
    owner_of = jnp.arange(batches, dtype=jnp.int32) // tile_count
    is_live = jnp.arange(capacity, dtype=jnp.int32)[None, :] < batch_counts.reshape(batches)[:, None]
    global_point = (wall_index + (owner_of * points)[:, None]).astype(jnp.int32)
    columns = wall_columns(flow_state)
    samples = jnp.take(columns, global_point.reshape(-1), axis=1)
    block_rows = tile_count * capacity
    sample_blocks = jnp.transpose(samples.reshape(14, owners, block_rows), (1, 0, 2))
    live_blocks = is_live.reshape(owners, block_rows).astype(jnp.float32)
    scale = grad_number / math.sqrt(SAMPLES)

    def step(carry, block):
        grad_in, grad_mid = carry
        rows, live_rows = block
        features = rows[:12].T
        targets = rows[12:].T.astype(jnp.float32)
        pre_first = jnp.dot(features, input_weight, preferred_element_type=jnp.float32)
        first_tanh = jnp.tanh(pre_first)
        first_act = first_tanh.astype(jnp.bfloat16)
        pre_second = jnp.dot(first_act, middle_weight, preferred_element_type=jnp.float32)
        second_tanh = jnp.tanh(pre_second)
        second_act = second_tanh.astype(jnp.bfloat16)
        prediction = jnp.dot(second_act, output_weight.T, preferred_element_type=jnp.float32)
        errors = (prediction - targets) * live_rows[:, None]
        back_out = (errors * scale).astype(jnp.bfloat16)
        back_second = (jnp.dot(back_out, output_weight, preferred_element_type=jnp.float32) * (1.0 - second_tanh * second_tanh)).astype(jnp.bfloat16)
        grad_mid = grad_mid + jnp.dot(first_act.T, back_second, preferred_element_type=jnp.float32)
        back_hidden = jnp.dot(back_second, middle_weight.T, preferred_element_type=jnp.float32)
        back_first = (back_hidden * (1.0 - first_tanh * first_tanh)).astype(jnp.bfloat16)
        grad_in = grad_in + jnp.dot(features.T, back_first, preferred_element_type=jnp.float32)
        return ((grad_in, grad_mid), (prediction.astype(jnp.bfloat16), lax.optimization_barrier(jnp.sum(errors * errors, axis=1))))
    init = (jnp.zeros((12, H), jnp.float32), jnp.zeros((H, H), jnp.float32))
    (grad_w_in, grad_w_mid), (sent, squares) = lax.scan(step, init, (sample_blocks, live_blocks))
    sent = sent.reshape(batches * capacity, 2)
    batch_sq = lax.optimization_barrier(jnp.sum(squares.reshape(batches, capacity), axis=1))
    route_flat = batch_routes.reshape(batches)
    matches = route_flat[:, None] == jnp.arange(owners, dtype=jnp.int32)[None, :]
    loss_sum = lax.optimization_barrier(jnp.sum(jnp.where(matches, batch_sq[:, None], jnp.zeros((), jnp.float32)), axis=0))
    count_float = batch_counts.reshape(batches).astype(jnp.float32)
    live_count = lax.optimization_barrier(jnp.sum(jnp.where(matches, count_float[:, None], jnp.zeros((), jnp.float32)), axis=0))
    batch_loss = 0.5 * loss_sum / live_count
    total_points = wall_stress.shape[1] * wall_stress.shape[2]
    target_index = jnp.where(is_live, global_point, total_points).reshape(-1)
    new_stress = wall_stress.reshape(2, total_points).at[:, target_index].set(sent.astype(jnp.float32).T, mode='drop').reshape(wall_stress.shape)
    below_z = jnp.roll(flow_state, 1, axis=2)
    above_z = jnp.roll(flow_state, -1, axis=2)
    advanced = advance(flow_state, diffusion, below_z, above_z)
    new_field = apply_wall(advanced, new_stress)
    return (new_field, new_stress, batch_loss, grad_w_in, grad_w_mid)
```

```python
import functools
import math

import jax
import jax.numpy as jnp
from jax import lax
from jax.experimental import pallas as pl
from jax.experimental.pallas import tpu as pltpu
from jax.sharding import Mesh, PartitionSpec as P

CORES = 2
LANE = 128

advect_number = 0.3
wall_gain = 0.5
grad_number = 32.0

FEATURES = 12
CHANNELS = 14
ROWS = 16

CHIPS = ("sec", "chip")
EVERY = ("sec", "chip", "core")

NN = (((1,), (0,)), ((), ()))
NT = (((1,), (1,)), ((), ()))
TN = (((0,), (0,)), ((), ()))


def mm(left, right, dims=NN):
    return lax.dot_general(left, right, dims, preferred_element_type=jnp.float32)


def round_up(value, step):
    return -(-value // step) * step


def iota(shape, axis):
    return lax.broadcasted_iota(jnp.int32, shape, axis)


def params(mib, **more):
    return pltpu.CompilerParams(vmem_limit_bytes=mib << 20, **more)


def pick_kernel(counts_ref, routes_ref, index_ref, flow_ref, rows_ref, info_ref, *, nx, capacity):
    tiles = counts_ref.shape[1]
    nz = flow_ref.shape[2]
    lanes = rows_ref.shape[1]
    shift = nx.bit_length() - 1
    counts = counts_ref[...].astype(jnp.float32)
    row, col = iota((tiles, tiles), 0), iota((tiles, tiles), 1)
    wide = jnp.broadcast_to(counts, (tiles, tiles))
    before = jnp.sum(jnp.where(col < row, wide, 0.0), axis=1, keepdims=True)
    own = jnp.sum(jnp.where(col == row, wide, 0.0), axis=1, keepdims=True)
    place = iota((tiles, lanes), 1).astype(jnp.float32)
    index = index_ref[...].astype(jnp.float32)
    routes = routes_ref[...].astype(jnp.float32)
    point = jnp.full((1, lanes), -1.0, jnp.float32)
    route = jnp.full((1, lanes), -1.0, jnp.float32)
    for k in range(capacity):
        here = (place == before + k) & (own > k)
        point = point + jnp.sum(
            jnp.where(here, index[:, k : k + 1] + 1.0, 0.0), axis=0, keepdims=True
        )
        route = route + jnp.sum(jnp.where(here, routes + 1.0, 0.0), axis=0, keepdims=True)
    point = point.astype(jnp.int32)
    info_ref[...] = jnp.concatenate(
        [point, route.astype(jnp.int32), jnp.full((6, lanes), -1, jnp.int32)], axis=0
    )
    at_z = lax.shift_right_arithmetic(point, shift)
    at_x = jnp.where(point < 0, -1, point & (nx - 1))
    hot_x = jnp.where(iota((nx, lanes), 0) == at_x, 1.0, 0.0).astype(jnp.bfloat16)
    hot_z = iota((nz, lanes), 0) == at_z

    def select(plane):
        near = mm(plane.astype(jnp.bfloat16), hot_x)
        return jnp.sum(jnp.where(hot_z, near, 0.0), axis=0, keepdims=True)

    out = [select(flow_ref[v, l]) for v in range(4) for l in range(3)]
    out += [select(flow_ref[v, 4] - flow_ref[v, 3]) for v in (1, 3)]
    out.append(jnp.zeros((ROWS - CHANNELS, lanes), jnp.float32))
    rows_ref[...] = jnp.concatenate(out, axis=0).astype(jnp.bfloat16)


def pick_samples(counts, routes, index, flow, lanes):
    tiles, capacity = index.shape
    nz, nx = flow.shape[2:]
    assert nx & (nx - 1) == 0
    whole = lambda shape: pl.BlockSpec(shape, lambda i: (0,) * len(shape))
    return pl.pallas_call(
        functools.partial(pick_kernel, nx=nx, capacity=capacity),
        grid=(1,),
        in_specs=[
            whole((1, tiles)),
            whole((tiles, 1)),
            whole((tiles, capacity)),
            whole((4, 5, nz, nx)),
        ],
        out_specs=[whole((ROWS, lanes)), whole((8, lanes))],
        out_shape=[
            jax.ShapeDtypeStruct((ROWS, lanes), jnp.bfloat16),
            jax.ShapeDtypeStruct((8, lanes), jnp.int32),
        ],
        compiler_params=params(32),
        name="pick",
    )(counts, routes, index, flow)


def assemble(core_ref, mine_ref, other_ref, weight_ref):
    core = core_ref[0]
    chips, rows, _ = mine_ref.shape
    for j in range(chips):
        at = pl.multiple_of((2 * j + core) * rows, rows)
        weight_ref[pl.ds(at, rows), :] = mine_ref[j]
        at = pl.multiple_of((2 * j + 1 - core) * rows, rows)
        weight_ref[pl.ds(at, rows), :] = other_ref[j]


def features_of(rows_ref):
    parts = [rows_ref[i] for i in range(rows_ref.shape[0])]
    across = parts[0] if len(parts) == 1 else jnp.concatenate(parts, axis=1)
    across = across.astype(jnp.float32)
    features = jnp.where(iota(across.shape, 0) < FEATURES, across, 0.0)
    return across, features


def forward_kernel(core_ref, rows_ref, mine_ref, other_ref, win_ref, wout_ref, second_ref, pred_ref, weight_ref, *, step):
    @pl.when(pl.program_id(0) == 0)
    def _():
        assemble(core_ref, mine_ref, other_ref, weight_ref)

    hidden = weight_ref.shape[0]
    _, features = features_of(rows_ref)
    tall = features.T.astype(jnp.bfloat16)
    total = None
    for at in range(0, hidden, step):
        first = jnp.tanh(mm(tall, win_ref[:, at : at + step])).astype(jnp.bfloat16)
        term = mm(first, weight_ref[at : at + step, :])
        total = term if total is None else total + term
    second = jnp.tanh(total).T
    second_ref[...] = second
    pred_ref[...] = mm(wout_ref[...], second.astype(jnp.bfloat16))


def forward(core, rows, mine, other, win, wout, group):
    chips, rows_dev, width = mine.shape
    lanes = rows.shape[2]
    hidden = win.shape[1]
    tile = group * lanes
    return pl.pallas_call(
        functools.partial(forward_kernel, step=min(hidden, 512)),
        grid=(chips // group,),
        in_specs=[
            pl.BlockSpec(memory_space=pltpu.SMEM),
            pl.BlockSpec((group, ROWS, lanes), lambda i: (i, 0, 0)),
            pl.BlockSpec(mine.shape, lambda i: (0, 0, 0)),
            pl.BlockSpec(other.shape, lambda i: (0, 0, 0)),
            pl.BlockSpec(win.shape, lambda i: (0, 0)),
            pl.BlockSpec(wout.shape, lambda i: (0, 0)),
        ],
        out_specs=[
            pl.BlockSpec((width, tile), lambda i: (0, i)),
            pl.BlockSpec((wout.shape[0], tile), lambda i: (0, i)),
        ],
        out_shape=[
            jax.ShapeDtypeStruct((width, chips * lanes), jnp.float32),
            jax.ShapeDtypeStruct((wout.shape[0], chips * lanes), jnp.float32),
        ],
        scratch_shapes=[pltpu.VMEM((hidden, width), jnp.bfloat16)],
        compiler_params=params(48),
        name="forward",
    )(core, rows, mine, other, win, wout)


def backward_kernel(
    core_ref, rows_ref, mine_ref, other_ref, win_ref, wout_ref, second_ref, pred_ref,
    keep_ref, send_ref, gin_ref, weight_ref, grad_ref, *, step, live, lanes, scale,
):
    i = pl.program_id(0)

    @pl.when(i == 0)
    def _():
        assemble(core_ref, mine_ref, other_ref, weight_ref)
        grad_ref[...] = jnp.zeros_like(grad_ref)
        gin_ref[...] = jnp.zeros_like(gin_ref)

    hidden = weight_ref.shape[0]
    across, features = features_of(rows_ref)
    tile = across.shape[1]
    counted = (iota((1, tile), 1) & (lanes - 1)) < live
    errors = jnp.where(counted, pred_ref[...] - across[FEATURES:CHANNELS], 0.0)
    back_out = (errors * scale).astype(jnp.bfloat16)
    second = second_ref[...]
    back = mm(wout_ref[...], back_out, TN) * (1.0 - second * second)
    across_back = back.astype(jnp.bfloat16)
    tall_back = back.T.astype(jnp.bfloat16)
    wide = features.astype(jnp.bfloat16)
    tall = features.T.astype(jnp.bfloat16)
    for at in range(0, hidden, step):
        act = jnp.tanh(mm(tall, win_ref[:, at : at + step]))
        grad_ref[:, at : at + step] += mm(across_back, act.astype(jnp.bfloat16))
        back_hidden = mm(tall_back, weight_ref[at : at + step, :], NT)
        back_first = (back_hidden * (1.0 - act * act)).astype(jnp.bfloat16)
        gin_ref[:, at : at + step] += mm(wide, back_first)

    @pl.when(i == pl.num_programs(0) - 1)
    def _():
        core = core_ref[0]
        chips, rows, _ = keep_ref.shape
        for j in range(chips):
            pair = grad_ref[:, 2 * j * rows : 2 * (j + 1) * rows].T
            low, high = pair[:rows], pair[rows:]
            keep_ref[j] = jnp.where(core == 0, low, high)
            send_ref[j] = jnp.where(core == 0, high, low)


def backward(core, rows, mine, other, win, wout, second, pred, group, live, scale):
    chips, rows_dev, width = mine.shape
    lanes = rows.shape[2]
    hidden = win.shape[1]
    tile = group * lanes
    assert lanes & (lanes - 1) == 0
    out3 = pl.BlockSpec(mine.shape, lambda i: (0, 0, 0))
    return pl.pallas_call(
        functools.partial(
            backward_kernel, step=min(hidden, 512), live=live, lanes=lanes, scale=scale
        ),
        grid=(chips // group,),
        in_specs=[
            pl.BlockSpec(memory_space=pltpu.SMEM),
            pl.BlockSpec((group, ROWS, lanes), lambda i: (i, 0, 0)),
            pl.BlockSpec(mine.shape, lambda i: (0, 0, 0)),
            pl.BlockSpec(other.shape, lambda i: (0, 0, 0)),
            pl.BlockSpec(win.shape, lambda i: (0, 0)),
            pl.BlockSpec(wout.shape, lambda i: (0, 0)),
            pl.BlockSpec((width, tile), lambda i: (0, i)),
            pl.BlockSpec((wout.shape[0], tile), lambda i: (0, i)),
        ],
        out_specs=[out3, out3, pl.BlockSpec((ROWS, hidden), lambda i: (0, 0))],
        out_shape=[
            jax.ShapeDtypeStruct(mine.shape, jnp.float32),
            jax.ShapeDtypeStruct(mine.shape, jnp.float32),
            jax.ShapeDtypeStruct((ROWS, hidden), jnp.float32),
        ],
        scratch_shapes=[
            pltpu.VMEM((hidden, width), jnp.bfloat16),
            pltpu.VMEM((width, hidden), jnp.float32),
        ],
        compiler_params=params(56),
        name="backward",
    )(core, rows, mine, other, win, wout, second, pred)


def slab_kernel(flow_ref, diff_ref, below_ref, above_ref, out_ref):
    layers, nz, nx = flow_ref.shape[1:]
    at_z, at_x = iota((nz, nx), 0), iota((nz, nx), 1)
    first_z, last_z = at_z == 0, at_z == nz - 1
    first_x, last_x = at_x == 0, at_x == nx - 1
    below_edge = below_ref[0].astype(jnp.float32)
    above_edge = above_ref[0].astype(jnp.float32)
    for l in range(layers):
        mid = flow_ref[0, l]
        below_x = jnp.where(first_x, mid, pltpu.roll(mid, 1, 1))
        above_x = jnp.where(last_x, mid, pltpu.roll(mid, nx - 1, 1))
        below_z = jnp.where(first_z, below_edge[l : l + 1], pltpu.roll(mid, 1, 0))
        above_z = jnp.where(last_z, above_edge[l : l + 1], pltpu.roll(mid, nz - 1, 0))
        below_y = flow_ref[0, max(l - 1, 0)]
        above_y = flow_ref[0, min(l + 1, layers - 1)]
        spread = below_x + above_x + below_y + above_y + below_z + above_z - 6.0 * mid
        out_ref[0, l] = mid + advect_number * (below_x - mid) + diff_ref[l] * spread


def slab(flow, diff, below, above):
    vars_, layers, nz, nx = flow.shape
    block = pl.BlockSpec((1, layers, nz, nx), lambda v: (v, 0, 0, 0))
    edge = pl.BlockSpec((1, layers, nx), lambda v: (v, 0, 0))
    return pl.pallas_call(
        slab_kernel,
        grid=(vars_,),
        in_specs=[block, pl.BlockSpec((layers, nz, nx), lambda v: (0, 0, 0)), edge, edge],
        out_specs=block,
        out_shape=jax.ShapeDtypeStruct(flow.shape, flow.dtype),
        compiler_params=params(32),
        name="slab",
    )(flow, diff, below, above)


def wall_kernel(info_ref, pred_ref, stress_ref, field_ref, stress_out, field_out):
    nz, nx = stress_ref.shape[1:]
    lanes = info_ref.shape[1]
    shift = nx.bit_length() - 1
    point = info_ref[0:1, :]
    at_z = lax.shift_right_arithmetic(point, shift)
    at_x = jnp.where(point < 0, -1, point & (nx - 1))
    hot_x = jnp.where(iota((nx, lanes), 0) == at_x, 1.0, 0.0).astype(jnp.bfloat16)
    hot_z = jnp.where(iota((nz, lanes), 0) == at_z, 1.0, 0.0)
    mask = jnp.broadcast_to(point >= 0, hot_z.shape)
    hit = mm(hot_z.astype(jnp.bfloat16), hot_x, NT)
    sent = jnp.where(pl.program_id(0) == 0, pred_ref[0:1, :], pred_ref[1:2, :])
    put = jnp.where(mask, hot_z * sent, 0.0).astype(jnp.bfloat16)
    fresh = jnp.where(hit > 0.5, mm(put, hot_x, NT), stress_ref[0])
    stress_out[0] = fresh
    field_out[0, 0] = field_ref[0, 0] - wall_gain * fresh


def wall(info, pred, stress, field):
    nz, nx = stress.shape[1:]
    lanes = info.shape[1]
    plane = pl.BlockSpec((1, nz, nx), lambda i: (i, 0, 0))
    layer = pl.BlockSpec((1, 1, nz, nx), lambda i: (2 * i + 1, 0, 0, 0))
    return pl.pallas_call(
        wall_kernel,
        grid=(2,),
        in_specs=[
            pl.BlockSpec((8, lanes), lambda i: (0, 0)),
            pl.BlockSpec((2, lanes), lambda i: (0, 0)),
            plane,
            layer,
        ],
        out_specs=[plane, layer],
        out_shape=[
            jax.ShapeDtypeStruct(stress.shape, stress.dtype),
            jax.ShapeDtypeStruct(field.shape, field.dtype),
        ],
        input_output_aliases={3: 1},
        compiler_params=params(16),
        name="wall",
    )(info, pred, stress, field)


def swap_cores(block):
    return lax.ppermute(block, "core", [(0, 1), (1, 0)])


def flip(block, mask, chips):
    return lax.ppermute(block, CHIPS, [(i, i ^ mask) for i in range(chips)])


def sum_chips(block, chips):
    mask = 1
    while mask < chips:
        if 2 * mask < chips:
            one, two, three = (flip(block, k * mask, chips) for k in (1, 2, 3))
            block = (block + one) + (two + three)
        else:
            block = block + flip(block, mask, chips)
        mask *= 4
    return block


def exchange(blocks):
    return lax.all_to_all(blocks, CHIPS, split_axis=0, concat_axis=0, tiled=True)


def body(
    flow_state,
    diffusion,
    wall_stress,
    batch_counts,
    batch_routes,
    wall_index,
    input_weight,
    middle_weight,
    output_weight,
):
    tile_count, capacity = wall_index.shape
    chips = lax.axis_size(CHIPS)
    devices = chips * CORES
    assert chips & (chips - 1) == 0
    chip, core = lax.axis_index(CHIPS), lax.axis_index("core")
    rows_dev, hidden = middle_weight.shape
    width = hidden // chips
    live_dev = 5 * tile_count * capacity // 8
    lanes = LANE
    while lanes < live_dev:
        lanes *= 2
    group = max(1, 512 // lanes)
    scale = grad_number / math.sqrt(live_dev * devices)

    order = [(i, (i + 1) % devices) for i in range(devices)]
    back_order = [(b, a) for a, b in order]
    edges = flow_state.astype(jnp.bfloat16)
    below = lax.ppermute(edges[:, :, -1], EVERY, order)
    above = lax.ppermute(edges[:, :, 0], EVERY, back_order)

    own_rows, info = pick_samples(batch_counts, batch_routes, wall_index, flow_state, lanes)
    blocks = jnp.transpose(middle_weight.reshape(rows_dev, chips, width), (1, 0, 2))
    if lanes == width:
        shared = jnp.broadcast_to(own_rows[None], (chips, ROWS, lanes))
        got = exchange(jnp.concatenate([blocks, shared], axis=1))
        mine, rows = got[:, :rows_dev], got[:, rows_dev:]
    else:
        mine = exchange(blocks)
        rows = exchange(jnp.broadcast_to(own_rows[None], (chips, ROWS, lanes)))
    other = swap_cores(mine)

    win = jnp.pad(input_weight, ((0, ROWS - FEATURES), (0, 0)))
    wout = lax.dynamic_slice_in_dim(output_weight, chip * width, width, axis=1)
    core_word = core.astype(jnp.int32).reshape(1)
    second, part = forward(core_word, rows, mine, other, win, wout, group)
    pred = sum_chips(part, chips)

    keep, send, grad_in = backward(
        core_word, rows, mine, other, win, wout, second, pred, group, live_dev, scale
    )
    grad = exchange(keep + swap_cores(send))
    grad_w_mid = jnp.transpose(grad, (1, 0, 2)).reshape(rows_dev, hidden)

    own_pred = lax.dynamic_slice_in_dim(pred, chip * lanes, lanes, axis=1)
    errors = own_pred - own_rows[FEATURES:CHANNELS].astype(jnp.float32)
    squares = 0.5 * jnp.sum(errors * errors, axis=0)
    match = info[1][:, None] == jnp.arange(devices, dtype=jnp.int32)[None, :]
    loss = jnp.sum(jnp.where(match, squares[:, None], 0.0), axis=0)
    count = jnp.sum(match.astype(jnp.float32), axis=0)
    tail = jnp.pad(jnp.stack([loss, count]), ((0, ROWS - CHANNELS), (0, hidden - devices)))
    packed = jnp.concatenate([grad_in[:FEATURES], tail], axis=0)
    packed = packed + swap_cores(packed)
    packed = sum_chips(packed, chips)
    grad_w_in = packed[:FEATURES]
    mine_at = chip * CORES + core
    sums = lax.dynamic_slice(packed, (FEATURES, mine_at), (2, 1))
    batch_loss = sums[0] / sums[1]

    field = slab(flow_state, diffusion, below, above)
    new_stress, new_field = wall(info, own_pred, wall_stress, field)
    return (new_field, new_stress, batch_loss, grad_w_in, grad_w_mid)


def solution(mesh):
    sec, dev = mesh.shape["sec"], mesh.shape["dev"]
    inner = Mesh(mesh.devices.reshape(sec, dev // CORES, CORES), EVERY)
    in_specs = (
        P(None, None, EVERY, None),
        P(None, EVERY, None),
        P(None, EVERY, None),
        P(EVERY, None),
        P(EVERY, None),
        P(EVERY, None),
        P(),
        P(EVERY, None),
        P(),
    )
    out_specs = (
        P(None, None, EVERY, None),
        P(None, EVERY, None),
        P(EVERY),
        P(),
        P(EVERY, None),
    )
    return jax.shard_map(body, mesh=inner, in_specs=in_specs, out_specs=out_specs, check_vma=False)
```

```python
import functools
import math

import jax
import jax.numpy as jnp
from jax import lax
from jax.experimental import pallas as pl
from jax.experimental.pallas import tpu as pltpu
from jax.sharding import Mesh, PartitionSpec as P


CORES = 2
LANE = 128
TILE = 2048
STEP = 256
KEEP_BYTES = 16 << 20

advect_number = 0.3
wall_gain = 0.5
grad_number = 32.0

FEATURES = 12
CHANNELS = 14
ROWS = 16

CHIPS = ("sec", "chip")
EVERY = ("sec", "chip", "core")

NN = (((1,), (0,)), ((), ()))
NT = (((1,), (1,)), ((), ()))
TN = (((0,), (0,)), ((), ()))


def mm(left, right, dims=NN):
    return lax.dot_general(left, right, dims, preferred_element_type=jnp.float32)


def round_up(value, step):
    return -(-value // step) * step


def iota(shape, axis):
    return lax.broadcasted_iota(jnp.int32, shape, axis)


def params(mib, **more):
    return pltpu.CompilerParams(vmem_limit_bytes=mib << 20, **more)


def pick_kernel(
    counts_ref, routes_ref, index_ref, flow_ref, low_ref, high_ref, weight_ref,
    rows_ref, info_ref, first_ref, last_ref, *block_ref, nx,
):
    first_ref[...] = low_ref[:, :, 0].astype(jnp.bfloat16)
    last_ref[...] = high_ref[:, :, high_ref.shape[2] - 1].astype(jnp.bfloat16)
    tiles = counts_ref.shape[1]
    nz = flow_ref.shape[2]
    lanes = rows_ref.shape[2]
    shift = nx.bit_length() - 1
    counts = counts_ref[...].astype(jnp.float32)
    row, col = iota((tiles, tiles), 0), iota((tiles, tiles), 1)
    tall = jnp.sum(jnp.where(col == row, counts, 0.0), axis=1, keepdims=True)
    before = jnp.sum(jnp.where(row < col, tall, 0.0), axis=0, keepdims=True)
    place = iota((lanes, tiles), 0).astype(jnp.float32)
    index = index_ref[...].astype(jnp.float32) + 1.0
    routes = routes_ref[...].astype(jnp.float32) + 1.0
    point = jnp.full((lanes, 1), -1.0, jnp.float32)
    route = jnp.full((lanes, 1), -1.0, jnp.float32)
    for k in range(index_ref.shape[0]):
        here = (place == before + k) & (counts > k)
        point += jnp.sum(jnp.where(here, index[k : k + 1], 0.0), axis=1, keepdims=True)
        route += jnp.sum(jnp.where(here, routes, 0.0), axis=1, keepdims=True)
    side = iota((lanes, LANE), 1)
    both = jnp.where(side == 0, point, jnp.where(side == 1, route, -1.0))
    info = both.T[:8].astype(jnp.int32)
    info_ref[...] = info
    point = info[0:1]
    at_z = lax.shift_right_arithmetic(point, shift)
    at_x = jnp.where(point < 0, -1, point & (nx - 1))
    hot_x = jnp.where(iota((nx, lanes), 0) == at_x, 1.0, 0.0).astype(jnp.bfloat16)
    hot_z = iota((nz, lanes), 0) == at_z

    planes = [flow_ref[v, l] for v in range(4) for l in range(3)]
    planes += [flow_ref[v, 4] - flow_ref[v, 3] for v in (1, 3)]
    stack = jnp.concatenate([plane.astype(jnp.bfloat16) for plane in planes], axis=0)
    near = mm(stack, hot_x).reshape(CHANNELS, nz, lanes)
    found = jnp.sum(jnp.where(hot_z[None], near, 0.0), axis=1)
    spare = jnp.zeros((ROWS - CHANNELS, lanes), jnp.float32)
    packed = jnp.concatenate([found, spare], axis=0).astype(jnp.bfloat16)
    rows_ref[0] = packed
    if block_ref:
        chips, tall, width = block_ref[0].shape
        for j in range(chips):
            block_ref[0][j, : tall - ROWS] = weight_ref[:, j * width : (j + 1) * width]
            block_ref[0][j, tall - ROWS :] = packed


def whole(shape):
    return pl.BlockSpec(shape, lambda i: (0,) * len(shape))


def pick_samples(counts, routes, index, flow, weight, lanes, joint):
    capacity, tiles = index.shape
    nv, nl, nz, nx = flow.shape
    assert nx & (nx - 1) == 0 and nz % 8 == 0
    plane = jax.ShapeDtypeStruct((nv, nl, nx), jnp.bfloat16)
    outs = [
        jax.ShapeDtypeStruct((1, ROWS, lanes), jnp.bfloat16),
        jax.ShapeDtypeStruct((8, lanes), jnp.int32),
        plane,
        plane,
    ]
    if joint is not None:
        outs.append(jax.ShapeDtypeStruct(joint, jnp.bfloat16))
    return pl.pallas_call(
        functools.partial(pick_kernel, nx=nx),
        grid=(1,),
        in_specs=[
            whole((1, tiles)),
            whole((1, tiles)),
            whole((capacity, tiles)),
            whole((4, 5, nz, nx)),
            whole((nv, nl, 8, nx)),
            pl.BlockSpec((nv, nl, 8, nx), lambda i: (0, 0, nz // 8 - 1, 0)),
            whole(weight.shape),
        ],
        out_specs=[whole(out.shape) for out in outs],
        out_shape=outs,
        compiler_params=params(16),
        name="pick",
    )(counts, routes, index, flow, flow, flow, weight)


def widen_kernel(weight_ref, out_ref):
    out_ref[...] = jnp.zeros_like(out_ref)
    out_ref[:FEATURES] = weight_ref[...]


def widen(weight):
    shape = (ROWS, weight.shape[1])
    return pl.pallas_call(
        widen_kernel,
        grid=(1,),
        in_specs=[whole(weight.shape)],
        out_specs=whole(shape),
        out_shape=jax.ShapeDtypeStruct(shape, weight.dtype),
        compiler_params=params(4),
        name="widen",
    )(weight)


def features_of(rows_ref):
    blocks = [rows_ref[g] for g in range(rows_ref.shape[0])]
    across = blocks[0] if len(blocks) == 1 else jnp.concatenate(blocks, axis=1)
    across = across.astype(jnp.float32)
    return across, jnp.where(iota(across.shape, 0) < FEATURES, across, 0.0)


def forward_kernel(
    place_ref, got_ref, mine_ref, other_ref, win_ref, wout_ref,
    second_ref, pred_ref, rows_ref, weight_ref, *first_ref, step,
):
    @pl.when(pl.program_id(0) == 0)
    def _():
        core = place_ref[0]
        chips, rows, _ = mine_ref.shape
        for j in range(chips):
            at = pl.multiple_of((CORES * j + core) * rows, rows)
            weight_ref[pl.ds(at, rows), :] = mine_ref[j]
            at = pl.multiple_of((CORES * j + 1 - core) * rows, rows)
            weight_ref[pl.ds(at, rows), :] = other_ref[j]

    hidden = weight_ref.shape[0]
    rows_ref[...] = got_ref[...]
    _, features = features_of(got_ref)
    tall = features.T.astype(jnp.bfloat16)
    total = None
    for at in range(0, hidden, step):
        first = jnp.tanh(mm(tall, win_ref[:, at : at + step])).astype(jnp.bfloat16)
        if first_ref:
            first_ref[0][:, at : at + step] = first
        term = mm(first, weight_ref[at : at + step, :])
        total = term if total is None else total + term
    second = jnp.tanh(total).T
    second_ref[...] = second
    pred_ref[...] = mm(wout_ref[...], second.astype(jnp.bfloat16))


def forward(place, got, skip, mine, other, win, wout, rows_dev, group, keep):
    chips, _, width = mine.shape
    lanes = got.shape[2]
    hidden = win.shape[1]
    tile, samples = group * lanes, chips * lanes
    out_specs = [
        pl.BlockSpec((width, tile), lambda i: (0, i)),
        pl.BlockSpec((wout.shape[0], tile), lambda i: (0, i)),
        pl.BlockSpec((group, ROWS, lanes), lambda i: (i, 0, 0)),
        whole((hidden, width)),
    ]
    out_shape = [
        jax.ShapeDtypeStruct((width, samples), jnp.float32),
        jax.ShapeDtypeStruct((wout.shape[0], samples), jnp.float32),
        jax.ShapeDtypeStruct((chips, ROWS, lanes), got.dtype),
        jax.ShapeDtypeStruct((hidden, width), jnp.bfloat16),
    ]
    if keep:
        out_specs.append(pl.BlockSpec((tile, hidden), lambda i: (i, 0)))
        out_shape.append(jax.ShapeDtypeStruct((samples, hidden), jnp.bfloat16))
    return pl.pallas_call(
        functools.partial(forward_kernel, step=min(hidden, STEP)),
        grid=(chips // group,),
        in_specs=[
            pl.BlockSpec(memory_space=pltpu.SMEM),
            pl.BlockSpec((group, ROWS, lanes), lambda i: (i, skip, 0)),
            whole((chips, rows_dev, width)),
            whole((chips, rows_dev, width)),
            whole(win.shape),
            whole(wout.shape),
        ],
        out_specs=out_specs,
        out_shape=out_shape,
        compiler_params=params(28),
        name="forward",
    )(place, got, mine, other, win, wout)


def back_second(across, pred_ref, second_ref, wout_ref, lanes, live, scale):
    counted = (iota((1, across.shape[1]), 1) & (lanes - 1)) < live
    errors = jnp.where(counted, pred_ref[...] - across[FEATURES:CHANNELS], 0.0)
    back_out = (errors * scale).astype(jnp.bfloat16)
    second = second_ref[...]
    return mm(wout_ref[...], back_out, TN) * (1.0 - second * second)


def middle_kernel(
    place_ref, rows_ref, win_ref, wout_ref, second_ref, pred_ref, *refs, step, live, scale, kept
):
    first_ref = refs[0] if kept else None
    keep_ref, send_ref, grad_ref = refs[kept:]
    i = pl.program_id(0)

    @pl.when(i == 0)
    def _():
        grad_ref[...] = jnp.zeros_like(grad_ref)

    hidden = win_ref.shape[1]
    lanes = rows_ref.shape[2]
    across, features = features_of(rows_ref)
    back = back_second(across, pred_ref, second_ref, wout_ref, lanes, live, scale)
    across_back = back.astype(jnp.bfloat16)
    tall = features.T.astype(jnp.bfloat16)
    for at in range(0, hidden, step):
        if kept:
            first = first_ref[:, at : at + step]
        else:
            first = jnp.tanh(mm(tall, win_ref[:, at : at + step])).astype(jnp.bfloat16)
        grad_ref[:, at : at + step] += mm(across_back, first)

    @pl.when(i == pl.num_programs(0) - 1)
    def _():
        core = place_ref[0]
        chips, rows, _ = keep_ref.shape
        for j in range(chips):
            pair = grad_ref[:, CORES * j * rows : CORES * (j + 1) * rows].T
            low, high = pair[:rows], pair[rows:]
            keep_ref[j] = jnp.where(core == 0, low, high)
            send_ref[j] = jnp.where(core == 0, high, low)


def middle_gradient(place, rows, win, wout, second, pred, first, rows_dev, group, live, scale):
    chips, _, lanes = rows.shape
    hidden = win.shape[1]
    width = wout.shape[1]
    tile = group * lanes
    assert lanes & (lanes - 1) == 0
    kept = len(first)
    blocks = jax.ShapeDtypeStruct((chips, rows_dev, width), jnp.float32)
    return pl.pallas_call(
        functools.partial(
            middle_kernel, step=min(hidden, STEP), live=live, scale=scale, kept=kept
        ),
        grid=(chips // group,),
        in_specs=[
            pl.BlockSpec(memory_space=pltpu.SMEM),
            pl.BlockSpec((group, ROWS, lanes), lambda i: (i, 0, 0)),
            whole(win.shape),
            whole(wout.shape),
            pl.BlockSpec((width, tile), lambda i: (0, i)),
            pl.BlockSpec((wout.shape[0], tile), lambda i: (0, i)),
        ]
        + [pl.BlockSpec((tile, hidden), lambda i: (i, 0))] * kept,
        out_specs=[whole(blocks.shape), whole(blocks.shape)],
        out_shape=[blocks, blocks],
        scratch_shapes=[pltpu.VMEM((width, hidden), jnp.float32)],
        compiler_params=params(16),
        name="middle",
    )(place, rows, win, wout, second, pred, *first)


def input_kernel(
    place_ref, rows_ref, win_ref, wout_ref, weight_ref, second_ref, pred_ref, all_ref, own_ref,
    info_ref, stay_ref, send_ref, gin_ref, *, step, live, scale, devices,
):
    @pl.when(pl.program_id(0) == 0)
    def _():
        gin_ref[...] = jnp.zeros_like(gin_ref)
        lanes = info_ref.shape[1]
        at = pl.multiple_of(place_ref[1] * lanes, lanes)
        errors = all_ref[:, pl.ds(at, lanes)] - own_ref[0, FEATURES:CHANNELS].astype(jnp.float32)
        squares = 0.5 * jnp.sum(errors * errors, axis=0, keepdims=True)
        route = info_ref[1:2].astype(jnp.float32)
        side = iota((8, lanes), 0)
        both = jnp.where(side == 0, route, squares).T
        across = round_up(devices, LANE)
        match = both[:, 0:1] == iota((lanes, across), 1).astype(jnp.float32)
        loss = jnp.sum(jnp.where(match, both[:, 1:2], 0.0), axis=0, keepdims=True)
        count = jnp.sum(jnp.where(match, 1.0, 0.0), axis=0, keepdims=True)
        gin_ref[FEATURES:CHANNELS, :across] = jnp.concatenate([loss, count], axis=0)

    hidden = win_ref.shape[1]
    across, features = features_of(rows_ref)
    wide = features.astype(jnp.bfloat16)
    tall = features.T.astype(jnp.bfloat16)
    back = back_second(
        across, pred_ref, second_ref, wout_ref, rows_ref.shape[2], live, scale
    )
    tall_back = back.T.astype(jnp.bfloat16)
    for at in range(0, hidden, step):
        act = jnp.tanh(mm(tall, win_ref[:, at : at + step]))
        back_hidden = mm(tall_back, weight_ref[at : at + step, :], NT)
        back_first = (back_hidden * (1.0 - act * act)).astype(jnp.bfloat16)
        gin_ref[:, at : at + step] += mm(wide, back_first)

    @pl.when(pl.program_id(0) == pl.num_programs(0) - 1)
    def _():
        low, high = gin_ref[:, : hidden // CORES], gin_ref[:, hidden // CORES :]
        first = place_ref[0] == 0
        stay_ref[...] = jnp.where(first, low, high)
        send_ref[...] = jnp.where(first, high, low)


def input_gradient(
    place, rows, win, wout, weight, second, pred, own, info, group, live, scale, devices
):
    chips, _, lanes = rows.shape
    hidden, width = weight.shape
    tile = group * lanes
    half = jax.ShapeDtypeStruct((ROWS, hidden // CORES), jnp.float32)
    return pl.pallas_call(
        functools.partial(
            input_kernel, step=min(hidden, STEP), live=live, scale=scale, devices=devices
        ),
        grid=(chips // group,),
        in_specs=[
            pl.BlockSpec(memory_space=pltpu.SMEM),
            pl.BlockSpec((group, ROWS, lanes), lambda i: (i, 0, 0)),
            whole(win.shape),
            whole(wout.shape),
            whole(weight.shape),
            pl.BlockSpec((width, tile), lambda i: (0, i)),
            pl.BlockSpec((pred.shape[0], tile), lambda i: (0, i)),
            whole(pred.shape),
            whole(own.shape),
            whole(info.shape),
        ],
        out_specs=[whole(half.shape), whole(half.shape)],
        out_shape=[half, half],
        scratch_shapes=[pltpu.VMEM((ROWS, hidden), jnp.float32)],
        compiler_params=params(16),
        name="input",
    )(place, rows, win, wout, weight, second, pred, pred, own, info)


def join_kernel(place_ref, half_ref, rest_ref, gin_ref, loss_ref):
    first = place_ref[0] == 0
    half, rest = half_ref[...], rest_ref[...]
    low, high = jnp.where(first, half, rest), jnp.where(first, rest, half)
    across = low.shape[1]
    gin_ref[:, :across] = low[:FEATURES]
    gin_ref[:, across:] = high[:FEATURES]
    mine = iota((1, across), 1) == place_ref[1] * CORES + place_ref[0]
    loss = jnp.sum(jnp.where(mine, low[FEATURES : FEATURES + 1], 0.0), axis=1, keepdims=True)
    count = jnp.sum(jnp.where(mine, low[FEATURES + 1 : CHANNELS], 0.0), axis=1, keepdims=True)
    loss_ref[...] = loss / count


def join_halves(place, half, rest):
    across = half.shape[1] * CORES
    return pl.pallas_call(
        join_kernel,
        grid=(1,),
        in_specs=[pl.BlockSpec(memory_space=pltpu.SMEM), whole(half.shape), whole(rest.shape)],
        out_specs=[whole((FEATURES, across)), whole((1, 1))],
        out_shape=[
            jax.ShapeDtypeStruct((FEATURES, across), jnp.float32),
            jax.ShapeDtypeStruct((1, 1), jnp.float32),
        ],
        compiler_params=params(8),
        name="join",
    )(place, half, rest)


def lay_kernel(blocks_ref, out_ref):
    chips, _, width = blocks_ref.shape
    for j in range(chips):
        out_ref[:, j * width : (j + 1) * width] = blocks_ref[j]


def lay_rows(blocks):
    chips, rows, width = blocks.shape
    return pl.pallas_call(
        lay_kernel,
        grid=(1,),
        in_specs=[whole(blocks.shape)],
        out_specs=whole((rows, chips * width)),
        out_shape=jax.ShapeDtypeStruct((rows, chips * width), blocks.dtype),
        compiler_params=params(8),
        name="lay",
    )(blocks)


def slab_kernel(flow_ref, diff_ref, below_ref, above_ref, out_ref):
    layers, nz, nx = flow_ref.shape[1:]
    at_z, at_x = iota((nz, nx), 0), iota((nz, nx), 1)
    first_z, last_z = at_z == 0, at_z == nz - 1
    first_x, last_x = at_x == 0, at_x == nx - 1
    below_edge = below_ref[0].astype(jnp.float32)
    above_edge = above_ref[0].astype(jnp.float32)
    for l in range(layers):
        mid = flow_ref[0, l]
        below_x = jnp.where(first_x, mid, pltpu.roll(mid, 1, 1))
        above_x = jnp.where(last_x, mid, pltpu.roll(mid, nx - 1, 1))
        below_z = jnp.where(first_z, below_edge[l : l + 1], pltpu.roll(mid, 1, 0))
        above_z = jnp.where(last_z, above_edge[l : l + 1], pltpu.roll(mid, nz - 1, 0))
        below_y = flow_ref[0, max(l - 1, 0)]
        above_y = flow_ref[0, min(l + 1, layers - 1)]
        spread = below_x + above_x + below_y + above_y + below_z + above_z - 6.0 * mid
        out_ref[0, l] = mid + advect_number * (below_x - mid) + diff_ref[l] * spread


def slab(flow, diff, below, above):
    vars_, layers, nz, nx = flow.shape
    block = pl.BlockSpec((1, layers, nz, nx), lambda v: (v, 0, 0, 0))
    edge = pl.BlockSpec((1, layers, nx), lambda v: (v, 0, 0))
    return pl.pallas_call(
        slab_kernel,
        grid=(vars_,),
        in_specs=[block, pl.BlockSpec((layers, nz, nx), lambda v: (0, 0, 0)), edge, edge],
        out_specs=block,
        out_shape=jax.ShapeDtypeStruct(flow.shape, flow.dtype),
        compiler_params=params(16),
        name="slab",
    )(flow, diff, below, above)


def wall_kernel(place_ref, info_ref, pred_ref, stress_ref, field_ref, stress_out, field_out):
    nz, nx = stress_ref.shape[1:]
    lanes = info_ref.shape[1]
    shift = nx.bit_length() - 1
    point = info_ref[0:1, :]
    at_z = lax.shift_right_arithmetic(point, shift)
    at_x = jnp.where(point < 0, -1, point & (nx - 1))
    hot_x = jnp.where(iota((nx, lanes), 0) == at_x, 1.0, 0.0).astype(jnp.bfloat16)
    hot_z = jnp.where(iota((nz, lanes), 0) == at_z, 1.0, 0.0)
    mask = jnp.broadcast_to(point >= 0, hot_z.shape)
    hit = mm(hot_z.astype(jnp.bfloat16), hot_x, NT)
    at = pl.multiple_of(place_ref[1] * lanes, lanes)
    own = pred_ref[:, pl.ds(at, lanes)]
    sent = jnp.where(pl.program_id(0) == 0, own[0:1], own[1:2])
    put = jnp.where(mask, hot_z * sent, 0.0).astype(jnp.bfloat16)
    fresh = jnp.where(hit > 0.5, mm(put, hot_x, NT), stress_ref[0])
    stress_out[0] = fresh
    field_out[0, 0] = field_ref[0, 0] - wall_gain * fresh


def wall(place, info, pred, stress, field):
    nz, nx = stress.shape[1:]
    plane = pl.BlockSpec((1, nz, nx), lambda i: (i, 0, 0))
    layer = pl.BlockSpec((1, 1, nz, nx), lambda i: (2 * i + 1, 0, 0, 0))
    return pl.pallas_call(
        wall_kernel,
        grid=(2,),
        in_specs=[
            pl.BlockSpec(memory_space=pltpu.SMEM),
            whole(info.shape),
            whole(pred.shape),
            plane,
            layer,
        ],
        out_specs=[plane, layer],
        out_shape=[
            jax.ShapeDtypeStruct(stress.shape, stress.dtype),
            jax.ShapeDtypeStruct(field.shape, field.dtype),
        ],
        input_output_aliases={4: 1},
        compiler_params=params(16),
        name="wall",
    )(place, info, pred, stress, field)


def swap_cores(block):
    return lax.ppermute(block, "core", [(0, 1), (1, 0)])


def flip(block, mask, chips):
    return lax.ppermute(block, CHIPS, [(i, i ^ mask) for i in range(chips)])


def sum_chips(block, chips, most):
    mask = 1
    while mask < chips:
        fan = min(most, chips // mask)
        others = [flip(block, k * mask, chips) for k in range(1, fan)]
        if fan == 4:
            block = (block + others[0]) + (others[1] + others[2])
        else:
            block = block + others[0]
        mask *= fan
    return block


def exchange(blocks):
    return lax.all_to_all(blocks, CHIPS, split_axis=0, concat_axis=0, tiled=True)


def step(
    flow_state,
    diffusion,
    wall_stress,
    batch_counts,
    batch_routes,
    wall_index,
    input_weight,
    middle_weight,
    output_weight,
):
    tile_count, capacity = wall_index.shape
    chips = lax.axis_size(CHIPS)
    devices = chips * CORES
    assert chips & (chips - 1) == 0
    chip, core = lax.axis_index(CHIPS), lax.axis_index("core")
    rows_dev, hidden = middle_weight.shape
    width = hidden // chips
    live_dev = 5 * tile_count * capacity // 8
    lanes = LANE
    while lanes < live_dev:
        lanes *= 2
    group = max(1, min(chips, TILE // lanes))
    scale = grad_number / math.sqrt(live_dev * devices)

    order = [(i, (i + 1) % devices) for i in range(devices)]
    back_order = [(b, a) for a, b in order]
    place = jnp.stack([core, chip]).astype(jnp.int32)
    joint = lanes == width and rows_dev % ROWS == 0
    far = lambda array: pltpu.with_memory_space_constraint(array, pltpu.HBM)
    own, info, first_z, last_z, *blocks = pick_samples(
        far(batch_counts),
        far(batch_routes.reshape(1, tile_count)),
        far(wall_index.T),
        far(flow_state),
        far(middle_weight),
        lanes,
        (chips, rows_dev + ROWS, width) if joint else None,
    )
    below = lax.ppermute(last_z, EVERY, order)
    above = lax.ppermute(first_z, EVERY, back_order)
    if joint:
        mine = exchange(blocks[0])
        got, skip = mine, rows_dev // ROWS
    else:
        mine = exchange(
            jnp.transpose(middle_weight.reshape(rows_dev, chips, width), (1, 0, 2))
        )
        got, skip = None, 0
    if not joint:
        got = exchange(jnp.broadcast_to(own, (chips, ROWS, lanes)))
    other = swap_cores(mine)

    win = widen(input_weight)
    wout = lax.dynamic_slice_in_dim(output_weight, chip * width, width, axis=1)
    keep = chips * lanes * hidden * 2 <= KEEP_BYTES
    second, part, rows, weight, *first = forward(
        place, got, skip, mine, other, win, wout, rows_dev, group, keep
    )
    pred = sum_chips(part, chips, 4)

    stay, send = middle_gradient(
        place, rows, win, wout, second, pred, first, rows_dev, group, live_dev, scale
    )
    summed = stay + swap_cores(send)
    grad = exchange(summed)
    grad_w_mid = lay_rows(grad)

    stay, send = input_gradient(
        place, rows, win, wout, weight, second, pred, own, info, group, live_dev, scale, devices
    )
    half = stay + swap_cores(send)
    half = sum_chips(half, chips, 2)
    rest = swap_cores(half)
    grad_w_in, loss = join_halves(place, half, rest)
    batch_loss = loss.reshape(1)

    field = slab(flow_state, diffusion, below, above)
    new_stress, new_field = wall(place, info, pred, wall_stress, field)
    return (new_field, new_stress, batch_loss, grad_w_in, grad_w_mid)


def solution(mesh):
    sec, dev = mesh.shape["sec"], mesh.shape["dev"]
    inner = Mesh(mesh.devices.reshape(sec, dev // CORES, CORES), EVERY)
    in_specs = (
        P(None, None, EVERY, None),
        P(None, EVERY, None),
        P(None, EVERY, None),
        P(EVERY, None),
        P(EVERY, None),
        P(EVERY, None),
        P(),
        P(EVERY, None),
        P(),
    )
    out_specs = (
        P(None, None, EVERY, None),
        P(None, EVERY, None),
        P(EVERY),
        P(),
        P(EVERY, None),
    )
    return jax.shard_map(step, mesh=inner, in_specs=in_specs, out_specs=out_specs, check_vma=False)
```

```python
import functools
import math

import jax
import jax.numpy as jnp
from jax import lax
from jax.experimental import pallas as pl
from jax.experimental.pallas import tpu as pltpu
from jax.sharding import Mesh, PartitionSpec as P


CORES = 2
LANE = 128
TILE = 2048
STEP = 256
KEEP_BYTES = 16 << 20

advect_number = 0.3
wall_gain = 0.5
grad_number = 32.0

FEATURES = 12
CHANNELS = 14
ROWS = 16
TAIL = ROWS - FEATURES

CHIPS = ("sec", "chip")
EVERY = ("sec", "chip", "core")

NN = (((1,), (0,)), ((), ()))
NT = (((1,), (1,)), ((), ()))
TN = (((0,), (0,)), ((), ()))


def mm(left, right, dims=NN):
    return lax.dot_general(left, right, dims, preferred_element_type=jnp.float32)


def iota(shape, axis):
    return lax.broadcasted_iota(jnp.int32, shape, axis)


def params(mib, **more):
    return pltpu.CompilerParams(vmem_limit_bytes=mib << 20, **more)


def pick_kernel(
    counts_ref, routes_ref, index_ref, flow_ref, weight_ref, rows_ref, info_ref, *block_ref, nx
):
    tiles = counts_ref.shape[1]
    nz = flow_ref.shape[2]
    lanes = rows_ref.shape[2]
    shift = nx.bit_length() - 1
    counts = counts_ref[...].astype(jnp.float32)
    row, col = iota((tiles, tiles), 0), iota((tiles, tiles), 1)
    tall = jnp.sum(jnp.where(col == row, counts, 0.0), axis=1, keepdims=True)
    before = jnp.sum(jnp.where(row < col, tall, 0.0), axis=0, keepdims=True)
    place = iota((lanes, tiles), 0).astype(jnp.float32)
    index = index_ref[...].astype(jnp.float32) + 1.0
    routes = routes_ref[...].astype(jnp.float32) + 1.0
    point = jnp.full((lanes, 1), -1.0, jnp.float32)
    route = jnp.full((lanes, 1), -1.0, jnp.float32)
    for k in range(index_ref.shape[0]):
        here = (place == before + k) & (counts > k)
        point += jnp.sum(jnp.where(here, index[k : k + 1], 0.0), axis=1, keepdims=True)
        route += jnp.sum(jnp.where(here, routes, 0.0), axis=1, keepdims=True)
    side = iota((lanes, LANE), 1)
    both = jnp.where(side == 0, point, jnp.where(side == 1, route, -1.0))
    info = both.T[:8].astype(jnp.int32)
    info_ref[...] = info
    point = info[0:1]
    at_z = lax.shift_right_arithmetic(point, shift)
    at_x = jnp.where(point < 0, -1, point & (nx - 1))
    hot_x = jnp.where(iota((nx, lanes), 0) == at_x, 1.0, 0.0).astype(jnp.bfloat16)
    hot_z = iota((nz, lanes), 0) == at_z

    planes = [flow_ref[v, l] for v in range(4) for l in range(3)]
    planes += [flow_ref[v, 4] - flow_ref[v, 3] for v in (1, 3)]
    stack = jnp.concatenate([plane.astype(jnp.bfloat16) for plane in planes], axis=0)
    near = mm(stack, hot_x).reshape(CHANNELS, nz, lanes)
    found = jnp.sum(jnp.where(hot_z[None], near, 0.0), axis=1)
    spare = jnp.zeros((ROWS - CHANNELS, lanes), jnp.float32)
    packed = jnp.concatenate([found, spare], axis=0).astype(jnp.bfloat16)
    rows_ref[0] = packed
    if block_ref:
        chips, tall, width = block_ref[0].shape
        for j in range(chips):
            block_ref[0][j, : tall - ROWS] = weight_ref[:, j * width : (j + 1) * width]
            block_ref[0][j, tall - ROWS :] = packed


def whole(shape):
    return pl.BlockSpec(shape, lambda i: (0,) * len(shape))


def pick_samples(counts, routes, index, flow, weight, lanes, joint):
    capacity, tiles = index.shape
    nz, nx = flow.shape[2:]
    assert nx & (nx - 1) == 0
    outs = [
        jax.ShapeDtypeStruct((1, ROWS, lanes), jnp.bfloat16),
        jax.ShapeDtypeStruct((8, lanes), jnp.int32),
    ]
    if joint is not None:
        outs.append(jax.ShapeDtypeStruct(joint, jnp.bfloat16))
    return pl.pallas_call(
        functools.partial(pick_kernel, nx=nx),
        grid=(1,),
        in_specs=[
            whole((1, tiles)),
            whole((1, tiles)),
            whole((capacity, tiles)),
            whole((4, 5, nz, nx)),
            whole(weight.shape),
        ],
        out_specs=[whole(out.shape) for out in outs],
        out_shape=outs,
        compiler_params=params(10),
        name="pick",
    )(counts, routes, index, flow, weight)


def edge_kernel(low_ref, high_ref, first_ref, last_ref):
    first_ref[...] = low_ref[:, :, 0].astype(jnp.bfloat16)
    last_ref[...] = high_ref[:, :, high_ref.shape[2] - 1].astype(jnp.bfloat16)


def edge_planes(flow):
    nv, nl, nz, nx = flow.shape
    plane = jax.ShapeDtypeStruct((nv, nl, nx), jnp.bfloat16)
    return pl.pallas_call(
        edge_kernel,
        grid=(1,),
        in_specs=[
            whole((nv, nl, 8, nx)),
            pl.BlockSpec((nv, nl, 8, nx), lambda i: (0, 0, nz // 8 - 1, 0)),
        ],
        out_specs=[whole(plane.shape), whole(plane.shape)],
        out_shape=[plane, plane],
        compiler_params=params(8),
        name="edge",
    )(flow, flow)


def widen_kernel(weight_ref, out_ref):
    out_ref[...] = jnp.zeros_like(out_ref)
    out_ref[:FEATURES] = weight_ref[...]


def widen(weight):
    shape = (ROWS, weight.shape[1])
    return pl.pallas_call(
        widen_kernel,
        grid=(1,),
        in_specs=[whole(weight.shape)],
        out_specs=whole(shape),
        out_shape=jax.ShapeDtypeStruct(shape, weight.dtype),
        compiler_params=params(4),
        name="widen",
    )(weight)


def features_of(rows_ref):
    blocks = [rows_ref[g] for g in range(rows_ref.shape[0])]
    across = blocks[0] if len(blocks) == 1 else jnp.concatenate(blocks, axis=1)
    across = across.astype(jnp.float32)
    return across, jnp.where(iota(across.shape, 0) < FEATURES, across, 0.0)


def forward_kernel(
    place_ref, got_ref, mine_ref, other_ref, win_ref, wout_ref,
    second_ref, pred_ref, rows_ref, weight_ref, *first_ref, step,
):
    @pl.when(pl.program_id(0) == 0)
    def _():
        core = place_ref[0]
        chips, rows, _ = mine_ref.shape
        for j in range(chips):
            at = pl.multiple_of((CORES * j + core) * rows, rows)
            weight_ref[pl.ds(at, rows), :] = mine_ref[j]
            at = pl.multiple_of((CORES * j + 1 - core) * rows, rows)
            weight_ref[pl.ds(at, rows), :] = other_ref[j, :rows]

    hidden = weight_ref.shape[0]
    rows_ref[...] = got_ref[...]
    _, features = features_of(got_ref)
    tall = features.T.astype(jnp.bfloat16)
    total = None
    for at in range(0, hidden, step):
        first = jnp.tanh(mm(tall, win_ref[:, at : at + step])).astype(jnp.bfloat16)
        if first_ref:
            first_ref[0][:, at : at + step] = first
        term = mm(first, weight_ref[at : at + step, :])
        total = term if total is None else total + term
    second = jnp.tanh(total).T
    second_ref[...] = second
    pred_ref[...] = mm(wout_ref[...], second.astype(jnp.bfloat16))


def forward(place, got, skip, mine, other, win, wout, rows_dev, group, keep):
    chips, _, width = mine.shape
    lanes = got.shape[2]
    hidden = win.shape[1]
    tile, samples = group * lanes, chips * lanes
    out_specs = [
        pl.BlockSpec((width, tile), lambda i: (0, i)),
        pl.BlockSpec((wout.shape[0], tile), lambda i: (0, i)),
        pl.BlockSpec((group, ROWS, lanes), lambda i: (i, 0, 0)),
        whole((hidden, width)),
    ]
    out_shape = [
        jax.ShapeDtypeStruct((width, samples), jnp.float32),
        jax.ShapeDtypeStruct((wout.shape[0], samples), jnp.float32),
        jax.ShapeDtypeStruct((chips, ROWS, lanes), got.dtype),
        jax.ShapeDtypeStruct((hidden, width), jnp.bfloat16),
    ]
    if keep:
        out_specs.append(pl.BlockSpec((tile, hidden), lambda i: (i, 0)))
        out_shape.append(jax.ShapeDtypeStruct((samples, hidden), jnp.bfloat16))
    return pl.pallas_call(
        functools.partial(forward_kernel, step=min(hidden, STEP)),
        grid=(chips // group,),
        in_specs=[
            pl.BlockSpec(memory_space=pltpu.SMEM),
            pl.BlockSpec((group, ROWS, lanes), lambda i: (i, skip, 0)),
            whole((chips, rows_dev, width)),
            whole(other.shape),
            whole(win.shape),
            whole(wout.shape),
        ],
        out_specs=out_specs,
        out_shape=out_shape,
        compiler_params=params(20),
        name="forward",
    )(place, got, mine, other, win, wout)


def back_second(across, pred_ref, second_ref, wout_ref, lanes, live, scale):
    counted = (iota((1, across.shape[1]), 1) & (lanes - 1)) < live
    errors = jnp.where(counted, pred_ref[...] - across[FEATURES:CHANNELS], 0.0)
    back_out = (errors * scale).astype(jnp.bfloat16)
    second = second_ref[...]
    return mm(wout_ref[...], back_out, TN) * (1.0 - second * second)


def middle_kernel(
    place_ref, rows_ref, win_ref, wout_ref, second_ref, pred_ref, *refs, step, live, scale, kept
):
    first_ref = refs[0] if kept else None
    keep_ref, send_ref, grad_ref = refs[kept:]
    i = pl.program_id(0)

    @pl.when(i == 0)
    def _():
        grad_ref[...] = jnp.zeros_like(grad_ref)

    hidden = win_ref.shape[1]
    lanes = rows_ref.shape[2]
    across, features = features_of(rows_ref)
    back = back_second(across, pred_ref, second_ref, wout_ref, lanes, live, scale)
    across_back = back.astype(jnp.bfloat16)
    tall = features.T.astype(jnp.bfloat16)
    for at in range(0, hidden, step):
        if kept:
            first = first_ref[:, at : at + step]
        else:
            first = jnp.tanh(mm(tall, win_ref[:, at : at + step])).astype(jnp.bfloat16)
        grad_ref[:, at : at + step] += mm(across_back, first)

    @pl.when(i == pl.num_programs(0) - 1)
    def _():
        core = place_ref[0]
        chips, rows, _ = keep_ref.shape
        for j in range(chips):
            pair = grad_ref[:, CORES * j * rows : CORES * (j + 1) * rows].T
            low, high = pair[:rows], pair[rows:]
            keep_ref[j] = jnp.where(core == 0, low, high)
            send_ref[j] = jnp.where(core == 0, high, low)


def middle_gradient(place, rows, win, wout, second, pred, first, rows_dev, group, live, scale):
    chips, _, lanes = rows.shape
    hidden = win.shape[1]
    width = wout.shape[1]
    tile = group * lanes
    assert lanes & (lanes - 1) == 0
    kept = len(first)
    blocks = jax.ShapeDtypeStruct((chips, rows_dev, width), jnp.float32)
    return pl.pallas_call(
        functools.partial(
            middle_kernel, step=min(hidden, STEP), live=live, scale=scale, kept=kept
        ),
        grid=(chips // group,),
        in_specs=[
            pl.BlockSpec(memory_space=pltpu.SMEM),
            pl.BlockSpec((group, ROWS, lanes), lambda i: (i, 0, 0)),
            whole(win.shape),
            whole(wout.shape),
            pl.BlockSpec((width, tile), lambda i: (0, i)),
            pl.BlockSpec((wout.shape[0], tile), lambda i: (0, i)),
        ]
        + [pl.BlockSpec((tile, hidden), lambda i: (i, 0))] * kept,
        out_specs=[whole(blocks.shape), whole(blocks.shape)],
        out_shape=[blocks, blocks],
        scratch_shapes=[pltpu.VMEM((width, hidden), jnp.float32)],
        compiler_params=params(14),
        name="middle",
    )(place, rows, win, wout, second, pred, *first)


def input_kernel(
    place_ref, rows_ref, win_ref, wout_ref, weight_ref, second_ref, pred_ref, all_ref, own_ref,
    info_ref, stay_ref, send_ref, gin_ref, *, step, live, scale,
):
    @pl.when(pl.program_id(0) == 0)
    def _():
        gin_ref[...] = jnp.zeros_like(gin_ref)
        lanes = info_ref.shape[1]
        at = pl.multiple_of(place_ref[1] * lanes, lanes)
        errors = all_ref[:, pl.ds(at, lanes)] - own_ref[0, FEATURES:CHANNELS].astype(jnp.float32)
        squares = 0.5 * jnp.sum(errors * errors, axis=0, keepdims=True)
        route = info_ref[1:2].astype(jnp.float32)
        side = iota((8, lanes), 0)
        both = jnp.where(side == 0, route, squares).T
        match = both[:, 0:1] == iota((lanes, LANE), 1).astype(jnp.float32)
        loss = jnp.sum(jnp.where(match, both[:, 1:2], 0.0), axis=0, keepdims=True)
        count = jnp.sum(jnp.where(match, 1.0, 0.0), axis=0, keepdims=True)
        gin_ref[FEATURES:CHANNELS, :LANE] = jnp.concatenate([loss, count], axis=0)

    hidden = win_ref.shape[1]
    across, features = features_of(rows_ref)
    wide = features.astype(jnp.bfloat16)
    tall = features.T.astype(jnp.bfloat16)
    back = back_second(
        across, pred_ref, second_ref, wout_ref, rows_ref.shape[2], live, scale
    )
    tall_back = back.T.astype(jnp.bfloat16)
    for at in range(0, hidden, step):
        act = jnp.tanh(mm(tall, win_ref[:, at : at + step]))
        back_hidden = mm(tall_back, weight_ref[at : at + step, :], NT)
        back_first = (back_hidden * (1.0 - act * act)).astype(jnp.bfloat16)
        gin_ref[:, at : at + step] += mm(wide, back_first)

    @pl.when(pl.program_id(0) == pl.num_programs(0) - 1)
    def _():
        cuts = [gin_ref[:FEATURES, at : at + LANE] for at in range(0, hidden, LANE)]
        cut = len(cuts) // CORES
        tail = gin_ref[FEATURES : FEATURES + TAIL, :LANE]
        low = jnp.concatenate(cuts[:cut] + [tail], axis=0)
        high = jnp.concatenate(cuts[cut:] + [jnp.zeros_like(tail)], axis=0)
        first = place_ref[0] == 0
        stay_ref[...] = jnp.where(first, low, high)
        send_ref[...] = jnp.where(first, high, low)


def input_gradient(
    place, rows, win, wout, weight, second, pred, own, info, group, live, scale, devices
):
    chips, _, lanes = rows.shape
    hidden, width = weight.shape
    tile = group * lanes
    assert hidden % (CORES * LANE) == 0 and devices <= LANE
    half = jax.ShapeDtypeStruct(
        (FEATURES * (hidden // CORES // LANE) + TAIL, LANE), jnp.float32
    )
    return pl.pallas_call(
        functools.partial(input_kernel, step=min(hidden, STEP), live=live, scale=scale),
        grid=(chips // group,),
        in_specs=[
            pl.BlockSpec(memory_space=pltpu.SMEM),
            pl.BlockSpec((group, ROWS, lanes), lambda i: (i, 0, 0)),
            whole(win.shape),
            whole(wout.shape),
            whole(weight.shape),
            pl.BlockSpec((width, tile), lambda i: (0, i)),
            pl.BlockSpec((pred.shape[0], tile), lambda i: (0, i)),
            whole(pred.shape),
            whole(own.shape),
            whole(info.shape),
        ],
        out_specs=[whole(half.shape), whole(half.shape)],
        out_shape=[half, half],
        scratch_shapes=[pltpu.VMEM((ROWS, hidden), jnp.float32)],
        compiler_params=params(14),
        name="input",
    )(place, rows, win, wout, weight, second, pred, pred, own, info)


def join_kernel(place_ref, half_ref, rest_ref, gin_ref, loss_ref):
    first = place_ref[0] == 0
    half, rest = half_ref[...], rest_ref[...]
    low, high = jnp.where(first, half, rest), jnp.where(first, rest, half)
    count = (low.shape[0] - TAIL) // FEATURES
    for i, part in enumerate((low, high)):
        for j in range(count):
            at = (i * count + j) * LANE
            gin_ref[:, at : at + LANE] = part[j * FEATURES : (j + 1) * FEATURES]
    mine = iota((TAIL, LANE), 1) == place_ref[1] * CORES + place_ref[0]
    sums = jnp.sum(jnp.where(mine, low[count * FEATURES :], 0.0), axis=1, keepdims=True)
    loss, count = sums[0:1], sums[1:2]
    loss_ref[...] = loss / count


def join_halves(place, half, rest):
    across = (half.shape[0] - TAIL) // FEATURES * LANE * CORES
    return pl.pallas_call(
        join_kernel,
        grid=(1,),
        in_specs=[pl.BlockSpec(memory_space=pltpu.SMEM), whole(half.shape), whole(rest.shape)],
        out_specs=[whole((FEATURES, across)), whole((1, 1))],
        out_shape=[
            jax.ShapeDtypeStruct((FEATURES, across), jnp.float32),
            jax.ShapeDtypeStruct((1, 1), jnp.float32),
        ],
        compiler_params=params(8),
        name="join",
    )(place, half, rest)


def lay_kernel(blocks_ref, out_ref):
    chips, _, width = blocks_ref.shape
    for j in range(chips):
        out_ref[:, j * width : (j + 1) * width] = blocks_ref[j]


def lay_rows(blocks):
    chips, rows, width = blocks.shape
    return pl.pallas_call(
        lay_kernel,
        grid=(1,),
        in_specs=[whole(blocks.shape)],
        out_specs=whole((rows, chips * width)),
        out_shape=jax.ShapeDtypeStruct((rows, chips * width), blocks.dtype),
        compiler_params=params(8),
        name="lay",
    )(blocks)


def slab_kernel(flow_ref, diff_ref, out_ref):
    layers, nz, nx = flow_ref.shape[1:]
    at_z, at_x = iota((nz, nx), 0), iota((nz, nx), 1)
    first_z, last_z = at_z == 0, at_z == nz - 1
    first_x, last_x = at_x == 0, at_x == nx - 1
    for l in range(layers):
        mid = flow_ref[0, l]
        below_x = jnp.where(first_x, mid, pltpu.roll(mid, 1, 1))
        above_x = jnp.where(last_x, mid, pltpu.roll(mid, nx - 1, 1))
        below_z = jnp.where(first_z, 0.0, pltpu.roll(mid, 1, 0))
        above_z = jnp.where(last_z, 0.0, pltpu.roll(mid, nz - 1, 0))
        below_y = flow_ref[0, max(l - 1, 0)]
        above_y = flow_ref[0, min(l + 1, layers - 1)]
        spread = below_x + above_x + below_y + above_y + below_z + above_z - 6.0 * mid
        out_ref[0, l] = mid + advect_number * (below_x - mid) + diff_ref[l] * spread


def slab(flow, diff):
    vars_, layers, nz, nx = flow.shape
    block = pl.BlockSpec((1, layers, nz, nx), lambda v: (v, 0, 0, 0))
    return pl.pallas_call(
        slab_kernel,
        grid=(vars_,),
        in_specs=[block, pl.BlockSpec((layers, nz, nx), lambda v: (0, 0, 0))],
        out_specs=block,
        out_shape=jax.ShapeDtypeStruct(flow.shape, flow.dtype),
        compiler_params=params(8),
        name="slab",
    )(flow, diff)


def rim_kernel(below_ref, above_ref, diff_ref, field_ref, out_ref):
    low = pl.program_id(0) == 0
    rows = field_ref.shape[2]
    edge = jnp.where(low, below_ref[...], above_ref[...]).astype(jnp.float32)
    row = jnp.where(low, 0, rows - 1)
    hit = iota((rows, field_ref.shape[3]), 0) == row
    diff = jnp.where(hit, diff_ref[...], 0.0)
    out_ref[...] = field_ref[...] + diff[None] * edge[:, :, None, :]


def rim(below, above, diff, field):
    vars_, layers, nz, nx = field.shape
    assert nz % 8 == 0 and nz >= 16
    last = nz // 8 - 1
    block = pl.BlockSpec((vars_, layers, 8, nx), lambda i: (0, 0, i * last, 0))
    return pl.pallas_call(
        rim_kernel,
        grid=(2,),
        in_specs=[
            whole(below.shape),
            whole(above.shape),
            pl.BlockSpec((layers, 8, nx), lambda i: (0, i * last, 0)),
            block,
        ],
        out_specs=block,
        out_shape=jax.ShapeDtypeStruct(field.shape, field.dtype),
        input_output_aliases={3: 0},
        compiler_params=params(6),
        name="rim",
    )(below, above, diff, field)


def wall_kernel(place_ref, info_ref, pred_ref, stress_ref, field_ref, stress_out, field_out):
    nz, nx = stress_ref.shape[1:]
    lanes = info_ref.shape[1]
    shift = nx.bit_length() - 1
    point = info_ref[0:1, :]
    at_z = lax.shift_right_arithmetic(point, shift)
    at_x = jnp.where(point < 0, -1, point & (nx - 1))
    hot_x = jnp.where(iota((nx, lanes), 0) == at_x, 1.0, 0.0).astype(jnp.bfloat16)
    hot_z = jnp.where(iota((nz, lanes), 0) == at_z, 1.0, 0.0)
    mask = jnp.broadcast_to(point >= 0, hot_z.shape)
    hit = mm(hot_z.astype(jnp.bfloat16), hot_x, NT)
    at = pl.multiple_of(place_ref[1] * lanes, lanes)
    own = pred_ref[:, pl.ds(at, lanes)]
    sent = jnp.where(pl.program_id(0) == 0, own[0:1], own[1:2])
    put = jnp.where(mask, hot_z * sent, 0.0).astype(jnp.bfloat16)
    fresh = jnp.where(hit > 0.5, mm(put, hot_x, NT), stress_ref[0])
    stress_out[0] = fresh
    field_out[0, 0] = field_ref[0, 0] - wall_gain * fresh


def wall(place, info, pred, stress, field):
    nz, nx = stress.shape[1:]
    plane = pl.BlockSpec((1, nz, nx), lambda i: (i, 0, 0))
    layer = pl.BlockSpec((1, 1, nz, nx), lambda i: (2 * i + 1, 0, 0, 0))
    return pl.pallas_call(
        wall_kernel,
        grid=(2,),
        in_specs=[
            pl.BlockSpec(memory_space=pltpu.SMEM),
            whole(info.shape),
            whole(pred.shape),
            plane,
            layer,
        ],
        out_specs=[plane, layer],
        out_shape=[
            jax.ShapeDtypeStruct(stress.shape, stress.dtype),
            jax.ShapeDtypeStruct(field.shape, field.dtype),
        ],
        input_output_aliases={4: 1},
        compiler_params=params(16),
        name="wall",
    )(place, info, pred, stress, field)


def swap_cores(block):
    return lax.ppermute(block, "core", [(0, 1), (1, 0)])


def flip(block, mask, chips):
    return lax.ppermute(block, CHIPS, [(i, i ^ mask) for i in range(chips)])


def sum_chips(block, chips, fans):
    mask = 1
    for most in fans + fans[-1:] * chips:
        if mask == chips:
            break
        fan = min(most, chips // mask)
        others = [flip(block, k * mask, chips) for k in range(1, fan)]
        if fan == 4:
            block = (block + others[0]) + (others[1] + others[2])
        else:
            block = block + others[0]
        mask *= fan
    return block


def exchange(blocks):
    return lax.all_to_all(blocks, CHIPS, split_axis=0, concat_axis=0, tiled=True)


def step(
    flow_state,
    diffusion,
    wall_stress,
    batch_counts,
    batch_routes,
    wall_index,
    input_weight,
    middle_weight,
    output_weight,
):
    tile_count, capacity = wall_index.shape
    chips = lax.axis_size(CHIPS)
    devices = chips * CORES
    assert chips & (chips - 1) == 0
    chip, core = lax.axis_index(CHIPS), lax.axis_index("core")
    rows_dev, hidden = middle_weight.shape
    width = hidden // chips
    live_dev = 5 * tile_count * capacity // 8
    lanes = LANE
    while lanes < live_dev:
        lanes *= 2
    group = max(1, min(chips, TILE // lanes))
    scale = grad_number / math.sqrt(live_dev * devices)

    order = [(i, (i + 1) % devices) for i in range(devices)]
    back_order = [(b, a) for a, b in order]
    place = jnp.stack([core, chip]).astype(jnp.int32)
    joint = lanes == width and rows_dev % ROWS == 0
    far = lambda array: pltpu.with_memory_space_constraint(array, pltpu.HBM)
    own, info, *blocks = pick_samples(
        far(batch_counts),
        far(batch_routes.reshape(1, tile_count)),
        far(wall_index.T),
        far(flow_state),
        far(middle_weight),
        lanes,
        (chips, rows_dev + ROWS, width) if joint else None,
    )
    blocks = [far(b) for b in blocks]
    first_z, last_z = edge_planes(flow_state)
    below = lax.ppermute(last_z, EVERY, order)
    above = lax.ppermute(first_z, EVERY, back_order)
    if joint:
        mine = exchange(blocks[0])
        got, skip = mine, rows_dev // ROWS
    else:
        mine = exchange(
            jnp.transpose(middle_weight.reshape(rows_dev, chips, width), (1, 0, 2))
        )
        got, skip = None, 0
    if not joint:
        got = exchange(jnp.broadcast_to(own, (chips, ROWS, lanes)))
    other = pltpu.with_memory_space_constraint(swap_cores(mine), pltpu.VMEM)

    win = widen(input_weight)
    wout = lax.dynamic_slice_in_dim(output_weight, chip * width, width, axis=1)
    keep = chips * lanes * hidden * 2 <= KEEP_BYTES
    second, part, rows, weight, *first = forward(
        place, got, skip, mine, other, win, wout, rows_dev, group, keep
    )
    pred = sum_chips(part, chips, (4,))

    stay, send = middle_gradient(
        place, rows, win, wout, second, pred, first, rows_dev, group, live_dev, scale
    )
    summed = stay + swap_cores(send)
    grad = exchange(summed)
    grad_w_mid = lay_rows(grad)

    stay, send = input_gradient(
        place, rows, win, wout, weight, second, pred, own, info, group, live_dev, scale, devices
    )
    half = stay + swap_cores(send)
    half = sum_chips(half, chips, (4, 2))
    rest = swap_cores(half)
    grad_w_in, loss = join_halves(place, half, rest)
    batch_loss = loss.reshape(1)

    field = slab(flow_state, diffusion)
    field = rim(below, above, far(diffusion), field)
    new_stress, new_field = wall(place, info, pred, wall_stress, field)
    return (new_field, new_stress, batch_loss, grad_w_in, grad_w_mid)


def solution(mesh):
    sec, dev = mesh.shape["sec"], mesh.shape["dev"]
    inner = Mesh(mesh.devices.reshape(sec, dev // CORES, CORES), EVERY)
    in_specs = (
        P(None, None, EVERY, None),
        P(None, EVERY, None),
        P(None, EVERY, None),
        P(EVERY, None),
        P(EVERY, None),
        P(EVERY, None),
        P(),
        P(EVERY, None),
        P(),
    )
    out_specs = (
        P(None, None, EVERY, None),
        P(None, EVERY, None),
        P(EVERY),
        P(),
        P(EVERY, None),
    )
    return jax.shard_map(
        step, mesh=inner, in_specs=in_specs, out_specs=out_specs, check_vma=False
    )
```

```python
import functools
import math

import jax
import jax.numpy as jnp
from jax import lax
from jax.experimental import pallas as pl
from jax.experimental.pallas import tpu as pltpu
from jax.sharding import Mesh, PartitionSpec as P


CORES = 2
LANE = 128
TILE = 2048
STEP = 256
KEEP_BYTES = 16 << 20

advect_number = 0.3
wall_gain = 0.5
grad_number = 32.0

FEATURES = 12
CHANNELS = 14
ROWS = 16
TAIL = ROWS - FEATURES

CHIPS = ("sec", "chip")
EVERY = ("sec", "chip", "core")

NN = (((1,), (0,)), ((), ()))
NT = (((1,), (1,)), ((), ()))
TN = (((0,), (0,)), ((), ()))


def mm(left, right, dims=NN):
    return lax.dot_general(left, right, dims, preferred_element_type=jnp.float32)


def iota(shape, axis):
    return lax.broadcasted_iota(jnp.int32, shape, axis)


def params(mib, **more):
    return pltpu.CompilerParams(vmem_limit_bytes=mib << 20, **more)


def pick_kernel(
    counts_ref, routes_ref, index_ref, flow_ref, weight_ref, rows_ref, info_ref, *block_ref, nx
):
    tiles = counts_ref.shape[1]
    nz = flow_ref.shape[2]
    lanes = rows_ref.shape[2]
    shift = nx.bit_length() - 1
    counts = counts_ref[...].astype(jnp.float32)
    row, col = iota((tiles, tiles), 0), iota((tiles, tiles), 1)
    tall = jnp.sum(jnp.where(col == row, counts, 0.0), axis=1, keepdims=True)
    before = jnp.sum(jnp.where(row < col, tall, 0.0), axis=0, keepdims=True)
    place = iota((lanes, tiles), 0).astype(jnp.float32)
    index = index_ref[...].astype(jnp.float32) + 1.0
    routes = routes_ref[...].astype(jnp.float32) + 1.0
    point = jnp.full((lanes, 1), -1.0, jnp.float32)
    route = jnp.full((lanes, 1), -1.0, jnp.float32)
    for k in range(index_ref.shape[0]):
        here = (place == before + k) & (counts > k)
        point += jnp.sum(jnp.where(here, index[k : k + 1], 0.0), axis=1, keepdims=True)
        route += jnp.sum(jnp.where(here, routes, 0.0), axis=1, keepdims=True)
    side = iota((lanes, LANE), 1)
    both = jnp.where(side == 0, point, jnp.where(side == 1, route, -1.0))
    info = both.T[:8].astype(jnp.int32)
    info_ref[...] = info
    point = info[0:1]
    at_z = lax.shift_right_arithmetic(point, shift)
    at_x = jnp.where(point < 0, -1, point & (nx - 1))
    hot_x = jnp.where(iota((nx, lanes), 0) == at_x, 1.0, 0.0).astype(jnp.bfloat16)
    hot_z = iota((nz, lanes), 0) == at_z

    planes = [flow_ref[v, l] for v in range(4) for l in range(3)]
    planes += [flow_ref[v, 4] - flow_ref[v, 3] for v in (1, 3)]
    stack = jnp.concatenate([plane.astype(jnp.bfloat16) for plane in planes], axis=0)
    near = mm(stack, hot_x).reshape(CHANNELS, nz, lanes)
    found = jnp.sum(jnp.where(hot_z[None], near, 0.0), axis=1)
    spare = jnp.zeros((ROWS - CHANNELS, lanes), jnp.float32)
    packed = jnp.concatenate([found, spare], axis=0).astype(jnp.bfloat16)
    rows_ref[0] = packed
    if block_ref:
        chips, tall, width = block_ref[0].shape
        for j in range(chips):
            block_ref[0][j, : tall - ROWS] = weight_ref[:, j * width : (j + 1) * width]
            block_ref[0][j, tall - ROWS :] = packed


def whole(shape):
    return pl.BlockSpec(shape, lambda i: (0,) * len(shape))


def pick_samples(counts, routes, index, flow, weight, lanes, joint):
    capacity, tiles = index.shape
    nz, nx = flow.shape[2:]
    assert nx & (nx - 1) == 0
    outs = [
        jax.ShapeDtypeStruct((1, ROWS, lanes), jnp.bfloat16),
        jax.ShapeDtypeStruct((8, lanes), jnp.int32),
    ]
    if joint is not None:
        outs.append(jax.ShapeDtypeStruct(joint, jnp.bfloat16))
    return pl.pallas_call(
        functools.partial(pick_kernel, nx=nx),
        grid=(1,),
        in_specs=[
            whole((1, tiles)),
            whole((1, tiles)),
            whole((capacity, tiles)),
            whole((4, 5, nz, nx)),
            whole(weight.shape),
        ],
        out_specs=[whole(out.shape) for out in outs],
        out_shape=outs,
        compiler_params=params(10),
        name="pick",
    )(counts, routes, index, flow, weight)


def edge_kernel(low_ref, high_ref, first_ref, last_ref):
    first_ref[...] = low_ref[:, :, 0].astype(jnp.bfloat16)
    last_ref[...] = high_ref[:, :, high_ref.shape[2] - 1].astype(jnp.bfloat16)


def edge_planes(flow):
    nv, nl, nz, nx = flow.shape
    plane = jax.ShapeDtypeStruct((nv, nl, nx), jnp.bfloat16)
    return pl.pallas_call(
        edge_kernel,
        grid=(1,),
        in_specs=[
            whole((nv, nl, 8, nx)),
            pl.BlockSpec((nv, nl, 8, nx), lambda i: (0, 0, nz // 8 - 1, 0)),
        ],
        out_specs=[whole(plane.shape), whole(plane.shape)],
        out_shape=[plane, plane],
        compiler_params=params(8),
        name="edge",
    )(flow, flow)


def widen_kernel(weight_ref, out_ref):
    out_ref[...] = jnp.zeros_like(out_ref)
    out_ref[:FEATURES] = weight_ref[...]


def widen(weight):
    shape = (ROWS, weight.shape[1])
    return pl.pallas_call(
        widen_kernel,
        grid=(1,),
        in_specs=[whole(weight.shape)],
        out_specs=whole(shape),
        out_shape=jax.ShapeDtypeStruct(shape, weight.dtype),
        compiler_params=params(4),
        name="widen",
    )(weight)


def features_of(rows_ref):
    blocks = [rows_ref[g] for g in range(rows_ref.shape[0])]
    across = blocks[0] if len(blocks) == 1 else jnp.concatenate(blocks, axis=1)
    across = across.astype(jnp.float32)
    return across, jnp.where(iota(across.shape, 0) < FEATURES, across, 0.0)


def assemble(place_ref, mine_ref, other_ref, weight_ref):
    core = place_ref[0]
    chips, rows, _ = mine_ref.shape
    for j in range(chips):
        at = pl.multiple_of((CORES * j + core) * rows, rows)
        weight_ref[pl.ds(at, rows), :] = mine_ref[j]
        at = pl.multiple_of((CORES * j + 1 - core) * rows, rows)
        weight_ref[pl.ds(at, rows), :] = other_ref[j, :rows]


def first_kernel(got_ref, win_ref, rows_ref, first_ref, *, step):
    rows_ref[...] = got_ref[...]
    _, features = features_of(got_ref)
    tall = features.T.astype(jnp.bfloat16)
    for at in range(0, first_ref.shape[1], step):
        act = jnp.tanh(mm(tall, win_ref[:, at : at + step]))
        first_ref[:, at : at + step] = act.astype(jnp.bfloat16)


def first_layer(got, skip, win, group):
    chips, _, lanes = got.shape
    hidden = win.shape[1]
    tile, samples = group * lanes, chips * lanes
    return pl.pallas_call(
        functools.partial(first_kernel, step=min(hidden, STEP)),
        grid=(chips // group,),
        in_specs=[
            pl.BlockSpec((group, ROWS, lanes), lambda i: (i, skip, 0)),
            whole(win.shape),
        ],
        out_specs=[
            pl.BlockSpec((group, ROWS, lanes), lambda i: (i, 0, 0)),
            pl.BlockSpec((tile, hidden), lambda i: (i, 0)),
        ],
        out_shape=[
            jax.ShapeDtypeStruct((chips, ROWS, lanes), got.dtype),
            jax.ShapeDtypeStruct((samples, hidden), jnp.bfloat16),
        ],
        compiler_params=params(28),
        name="first",
    )(got, win)


def second_kernel(
    place_ref, first_ref, mine_ref, other_ref, wout_ref, second_ref, pred_ref, weight_ref
):
    @pl.when(pl.program_id(0) == 0)
    def _():
        assemble(place_ref, mine_ref, other_ref, weight_ref)

    second = jnp.tanh(mm(first_ref[...], weight_ref[...])).T
    second_ref[...] = second
    pred_ref[...] = mm(wout_ref[...], second.astype(jnp.bfloat16))


def second_layer(place, first, mine, other, wout, rows_dev, tile):
    chips, _, width = mine.shape
    samples, hidden = first.shape
    return pl.pallas_call(
        second_kernel,
        grid=(samples // tile,),
        in_specs=[
            pl.BlockSpec(memory_space=pltpu.SMEM),
            pl.BlockSpec((tile, hidden), lambda i: (i, 0)),
            whole((chips, rows_dev, width)),
            whole(other.shape),
            whole(wout.shape),
        ],
        out_specs=[
            pl.BlockSpec((width, tile), lambda i: (0, i)),
            pl.BlockSpec((wout.shape[0], tile), lambda i: (0, i)),
            whole((hidden, width)),
        ],
        out_shape=[
            jax.ShapeDtypeStruct((width, samples), jnp.float32),
            jax.ShapeDtypeStruct((wout.shape[0], samples), jnp.float32),
            jax.ShapeDtypeStruct((hidden, width), jnp.bfloat16),
        ],
        compiler_params=params(28),
        name="second",
    )(place, first, mine, other, wout)


def forward_kernel(
    place_ref, got_ref, mine_ref, other_ref, win_ref, wout_ref,
    second_ref, pred_ref, rows_ref, weight_ref, *, step,
):
    @pl.when(pl.program_id(0) == 0)
    def _():
        assemble(place_ref, mine_ref, other_ref, weight_ref)

    hidden = weight_ref.shape[0]
    rows_ref[...] = got_ref[...]
    _, features = features_of(got_ref)
    tall = features.T.astype(jnp.bfloat16)
    total = None
    for at in range(0, hidden, step):
        first = jnp.tanh(mm(tall, win_ref[:, at : at + step])).astype(jnp.bfloat16)
        term = mm(first, weight_ref[at : at + step, :])
        total = term if total is None else total + term
    second = jnp.tanh(total).T
    second_ref[...] = second
    pred_ref[...] = mm(wout_ref[...], second.astype(jnp.bfloat16))


def forward(place, got, skip, mine, other, win, wout, rows_dev, group):
    chips, _, width = mine.shape
    lanes = got.shape[2]
    hidden = win.shape[1]
    tile, samples = group * lanes, chips * lanes
    out_specs = [
        pl.BlockSpec((width, tile), lambda i: (0, i)),
        pl.BlockSpec((wout.shape[0], tile), lambda i: (0, i)),
        pl.BlockSpec((group, ROWS, lanes), lambda i: (i, 0, 0)),
        whole((hidden, width)),
    ]
    out_shape = [
        jax.ShapeDtypeStruct((width, samples), jnp.float32),
        jax.ShapeDtypeStruct((wout.shape[0], samples), jnp.float32),
        jax.ShapeDtypeStruct((chips, ROWS, lanes), got.dtype),
        jax.ShapeDtypeStruct((hidden, width), jnp.bfloat16),
    ]
    return pl.pallas_call(
        functools.partial(forward_kernel, step=min(hidden, STEP)),
        grid=(chips // group,),
        in_specs=[
            pl.BlockSpec(memory_space=pltpu.SMEM),
            pl.BlockSpec((group, ROWS, lanes), lambda i: (i, skip, 0)),
            whole((chips, rows_dev, width)),
            whole(other.shape),
            whole(win.shape),
            whole(wout.shape),
        ],
        out_specs=out_specs,
        out_shape=out_shape,
        compiler_params=params(20),
        name="forward",
    )(place, got, mine, other, win, wout)


def back_second(across, pred_ref, second_ref, wout_ref, lanes, live, scale):
    counted = (iota((1, across.shape[1]), 1) & (lanes - 1)) < live
    errors = jnp.where(counted, pred_ref[...] - across[FEATURES:CHANNELS], 0.0)
    back_out = (errors * scale).astype(jnp.bfloat16)
    second = second_ref[...]
    return mm(wout_ref[...], back_out, TN) * (1.0 - second * second)


def middle_kernel(
    place_ref, rows_ref, win_ref, wout_ref, second_ref, pred_ref, *refs, step, live, scale, kept
):
    first_ref = refs[0] if kept else None
    keep_ref, send_ref, grad_ref = refs[kept:]
    i = pl.program_id(0)

    @pl.when(i == 0)
    def _():
        grad_ref[...] = jnp.zeros_like(grad_ref)

    hidden = win_ref.shape[1]
    lanes = rows_ref.shape[2]
    across, features = features_of(rows_ref)
    back = back_second(across, pred_ref, second_ref, wout_ref, lanes, live, scale)
    across_back = back.astype(jnp.bfloat16)
    tall = features.T.astype(jnp.bfloat16)
    for at in range(0, hidden, step):
        if kept:
            first = first_ref[:, at : at + step]
        else:
            first = jnp.tanh(mm(tall, win_ref[:, at : at + step])).astype(jnp.bfloat16)
        grad_ref[:, at : at + step] += mm(across_back, first)

    @pl.when(i == pl.num_programs(0) - 1)
    def _():
        core = place_ref[0]
        chips, rows, _ = keep_ref.shape
        for j in range(chips):
            pair = grad_ref[:, CORES * j * rows : CORES * (j + 1) * rows].T
            low, high = pair[:rows], pair[rows:]
            keep_ref[j] = jnp.where(core == 0, low, high)
            send_ref[j] = jnp.where(core == 0, high, low)


def middle_gradient(place, rows, win, wout, second, pred, first, rows_dev, group, live, scale):
    chips, _, lanes = rows.shape
    hidden = win.shape[1]
    width = wout.shape[1]
    tile = group * lanes
    assert lanes & (lanes - 1) == 0
    kept = len(first)
    blocks = jax.ShapeDtypeStruct((chips, rows_dev, width), jnp.float32)
    return pl.pallas_call(
        functools.partial(
            middle_kernel, step=min(hidden, STEP), live=live, scale=scale, kept=kept
        ),
        grid=(chips // group,),
        in_specs=[
            pl.BlockSpec(memory_space=pltpu.SMEM),
            pl.BlockSpec((group, ROWS, lanes), lambda i: (i, 0, 0)),
            whole(win.shape),
            whole(wout.shape),
            pl.BlockSpec((width, tile), lambda i: (0, i)),
            pl.BlockSpec((wout.shape[0], tile), lambda i: (0, i)),
        ]
        + [pl.BlockSpec((tile, hidden), lambda i: (i, 0))] * kept,
        out_specs=[whole(blocks.shape), whole(blocks.shape)],
        out_shape=[blocks, blocks],
        scratch_shapes=[pltpu.VMEM((width, hidden), jnp.float32)],
        compiler_params=params(14),
        name="middle",
    )(place, rows, win, wout, second, pred, *first)


def input_kernel(
    place_ref, rows_ref, win_ref, wout_ref, weight_ref, second_ref, pred_ref, all_ref, own_ref,
    info_ref, stay_ref, send_ref, gin_ref, *, step, live, scale,
):
    @pl.when(pl.program_id(0) == 0)
    def _():
        gin_ref[...] = jnp.zeros_like(gin_ref)
        lanes = info_ref.shape[1]
        at = pl.multiple_of(place_ref[1] * lanes, lanes)
        errors = all_ref[:, pl.ds(at, lanes)] - own_ref[0, FEATURES:CHANNELS].astype(jnp.float32)
        squares = 0.5 * jnp.sum(errors * errors, axis=0, keepdims=True)
        route = info_ref[1:2].astype(jnp.float32)
        side = iota((8, lanes), 0)
        both = jnp.where(side == 0, route, squares).T
        match = both[:, 0:1] == iota((lanes, LANE), 1).astype(jnp.float32)
        loss = jnp.sum(jnp.where(match, both[:, 1:2], 0.0), axis=0, keepdims=True)
        count = jnp.sum(jnp.where(match, 1.0, 0.0), axis=0, keepdims=True)
        gin_ref[FEATURES:CHANNELS, :LANE] = jnp.concatenate([loss, count], axis=0)

    hidden = win_ref.shape[1]
    across, features = features_of(rows_ref)
    wide = features.astype(jnp.bfloat16)
    tall = features.T.astype(jnp.bfloat16)
    back = back_second(
        across, pred_ref, second_ref, wout_ref, rows_ref.shape[2], live, scale
    )
    tall_back = back.T.astype(jnp.bfloat16)
    for at in range(0, hidden, step):
        act = jnp.tanh(mm(tall, win_ref[:, at : at + step]))
        back_hidden = mm(tall_back, weight_ref[at : at + step, :], NT)
        back_first = (back_hidden * (1.0 - act * act)).astype(jnp.bfloat16)
        gin_ref[:, at : at + step] += mm(wide, back_first)

    @pl.when(pl.program_id(0) == pl.num_programs(0) - 1)
    def _():
        cuts = [gin_ref[:FEATURES, at : at + LANE] for at in range(0, hidden, LANE)]
        cut = len(cuts) // CORES
        tail = gin_ref[FEATURES : FEATURES + TAIL, :LANE]
        low = jnp.concatenate(cuts[:cut] + [tail], axis=0)
        high = jnp.concatenate(cuts[cut:] + [jnp.zeros_like(tail)], axis=0)
        first = place_ref[0] == 0
        stay_ref[...] = jnp.where(first, low, high)
        send_ref[...] = jnp.where(first, high, low)


def input_gradient(
    place, rows, win, wout, weight, second, pred, own, info, group, live, scale, devices
):
    chips, _, lanes = rows.shape
    hidden, width = weight.shape
    tile = group * lanes
    assert hidden % (CORES * LANE) == 0 and devices <= LANE
    half = jax.ShapeDtypeStruct(
        (FEATURES * (hidden // CORES // LANE) + TAIL, LANE), jnp.float32
    )
    return pl.pallas_call(
        functools.partial(input_kernel, step=min(hidden, STEP), live=live, scale=scale),
        grid=(chips // group,),
        in_specs=[
            pl.BlockSpec(memory_space=pltpu.SMEM),
            pl.BlockSpec((group, ROWS, lanes), lambda i: (i, 0, 0)),
            whole(win.shape),
            whole(wout.shape),
            whole(weight.shape),
            pl.BlockSpec((width, tile), lambda i: (0, i)),
            pl.BlockSpec((pred.shape[0], tile), lambda i: (0, i)),
            whole(pred.shape),
            whole(own.shape),
            whole(info.shape),
        ],
        out_specs=[whole(half.shape), whole(half.shape)],
        out_shape=[half, half],
        scratch_shapes=[pltpu.VMEM((ROWS, hidden), jnp.float32)],
        compiler_params=params(14),
        name="input",
    )(place, rows, win, wout, weight, second, pred, pred, own, info)


def join_kernel(place_ref, half_ref, rest_ref, gin_ref, loss_ref):
    first = place_ref[0] == 0
    half, rest = half_ref[...], rest_ref[...]
    low, high = jnp.where(first, half, rest), jnp.where(first, rest, half)
    count = (low.shape[0] - TAIL) // FEATURES
    for i, part in enumerate((low, high)):
        for j in range(count):
            at = (i * count + j) * LANE
            gin_ref[:, at : at + LANE] = part[j * FEATURES : (j + 1) * FEATURES]
    mine = iota((TAIL, LANE), 1) == place_ref[1] * CORES + place_ref[0]
    sums = jnp.sum(jnp.where(mine, low[count * FEATURES :], 0.0), axis=1, keepdims=True)
    loss, count = sums[0:1], sums[1:2]
    loss_ref[...] = loss / count


def join_halves(place, half, rest):
    across = (half.shape[0] - TAIL) // FEATURES * LANE * CORES
    return pl.pallas_call(
        join_kernel,
        grid=(1,),
        in_specs=[pl.BlockSpec(memory_space=pltpu.SMEM), whole(half.shape), whole(rest.shape)],
        out_specs=[whole((FEATURES, across)), whole((1, 1))],
        out_shape=[
            jax.ShapeDtypeStruct((FEATURES, across), jnp.float32),
            jax.ShapeDtypeStruct((1, 1), jnp.float32),
        ],
        compiler_params=params(8),
        name="join",
    )(place, half, rest)


def lay_kernel(blocks_ref, out_ref):
    chips, _, width = blocks_ref.shape
    for j in range(chips):
        out_ref[:, j * width : (j + 1) * width] = blocks_ref[j]


def lay_rows(blocks):
    chips, rows, width = blocks.shape
    return pl.pallas_call(
        lay_kernel,
        grid=(1,),
        in_specs=[whole(blocks.shape)],
        out_specs=whole((rows, chips * width)),
        out_shape=jax.ShapeDtypeStruct((rows, chips * width), blocks.dtype),
        compiler_params=params(8),
        name="lay",
    )(blocks)


def slab_kernel(flow_ref, diff_ref, out_ref):
    layers, nz, nx = flow_ref.shape[1:]
    at_z, at_x = iota((nz, nx), 0), iota((nz, nx), 1)
    first_z, last_z = at_z == 0, at_z == nz - 1
    first_x, last_x = at_x == 0, at_x == nx - 1
    for l in range(layers):
        mid = flow_ref[0, l]
        below_x = jnp.where(first_x, mid, pltpu.roll(mid, 1, 1))
        above_x = jnp.where(last_x, mid, pltpu.roll(mid, nx - 1, 1))
        below_z = jnp.where(first_z, 0.0, pltpu.roll(mid, 1, 0))
        above_z = jnp.where(last_z, 0.0, pltpu.roll(mid, nz - 1, 0))
        below_y = flow_ref[0, max(l - 1, 0)]
        above_y = flow_ref[0, min(l + 1, layers - 1)]
        spread = below_x + above_x + below_y + above_y + below_z + above_z - 6.0 * mid
        out_ref[0, l] = mid + advect_number * (below_x - mid) + diff_ref[l] * spread


def slab(flow, diff):
    vars_, layers, nz, nx = flow.shape
    block = pl.BlockSpec((1, layers, nz, nx), lambda v: (v, 0, 0, 0))
    return pl.pallas_call(
        slab_kernel,
        grid=(vars_,),
        in_specs=[block, pl.BlockSpec((layers, nz, nx), lambda v: (0, 0, 0))],
        out_specs=block,
        out_shape=jax.ShapeDtypeStruct(flow.shape, flow.dtype),
        compiler_params=params(8),
        name="slab",
    )(flow, diff)


def rim_kernel(below_ref, above_ref, diff_ref, field_ref, out_ref):
    low = pl.program_id(0) == 0
    rows = field_ref.shape[2]
    edge = jnp.where(low, below_ref[...], above_ref[...]).astype(jnp.float32)
    row = jnp.where(low, 0, rows - 1)
    hit = iota((rows, field_ref.shape[3]), 0) == row
    diff = jnp.where(hit, diff_ref[...], 0.0)
    out_ref[...] = field_ref[...] + diff[None] * edge[:, :, None, :]


def rim(below, above, diff, field):
    vars_, layers, nz, nx = field.shape
    assert nz % 8 == 0 and nz >= 16
    last = nz // 8 - 1
    block = pl.BlockSpec((vars_, layers, 8, nx), lambda i: (0, 0, i * last, 0))
    return pl.pallas_call(
        rim_kernel,
        grid=(2,),
        in_specs=[
            whole(below.shape),
            whole(above.shape),
            pl.BlockSpec((layers, 8, nx), lambda i: (0, i * last, 0)),
            block,
        ],
        out_specs=block,
        out_shape=jax.ShapeDtypeStruct(field.shape, field.dtype),
        input_output_aliases={3: 0},
        compiler_params=params(6),
        name="rim",
    )(below, above, diff, field)


def wall_kernel(place_ref, info_ref, pred_ref, stress_ref, field_ref, stress_out, field_out):
    nz, nx = stress_ref.shape[1:]
    lanes = info_ref.shape[1]
    shift = nx.bit_length() - 1
    point = info_ref[0:1, :]
    at_z = lax.shift_right_arithmetic(point, shift)
    at_x = jnp.where(point < 0, -1, point & (nx - 1))
    hot_x = jnp.where(iota((nx, lanes), 0) == at_x, 1.0, 0.0).astype(jnp.bfloat16)
    hot_z = jnp.where(iota((nz, lanes), 0) == at_z, 1.0, 0.0)
    mask = jnp.broadcast_to(point >= 0, hot_z.shape)
    hit = mm(hot_z.astype(jnp.bfloat16), hot_x, NT)
    at = pl.multiple_of(place_ref[1] * lanes, lanes)
    own = pred_ref[:, pl.ds(at, lanes)]
    sent = jnp.where(pl.program_id(0) == 0, own[0:1], own[1:2])
    put = jnp.where(mask, hot_z * sent, 0.0).astype(jnp.bfloat16)
    fresh = jnp.where(hit > 0.5, mm(put, hot_x, NT), stress_ref[0])
    stress_out[0] = fresh
    field_out[0, 0] = field_ref[0, 0] - wall_gain * fresh


def wall(place, info, pred, stress, field):
    nz, nx = stress.shape[1:]
    plane = pl.BlockSpec((1, nz, nx), lambda i: (i, 0, 0))
    layer = pl.BlockSpec((1, 1, nz, nx), lambda i: (2 * i + 1, 0, 0, 0))
    return pl.pallas_call(
        wall_kernel,
        grid=(2,),
        in_specs=[
            pl.BlockSpec(memory_space=pltpu.SMEM),
            whole(info.shape),
            whole(pred.shape),
            plane,
            layer,
        ],
        out_specs=[plane, layer],
        out_shape=[
            jax.ShapeDtypeStruct(stress.shape, stress.dtype),
            jax.ShapeDtypeStruct(field.shape, field.dtype),
        ],
        input_output_aliases={4: 1},
        compiler_params=params(16),
        name="wall",
    )(place, info, pred, stress, field)


def swap_cores(block):
    return lax.ppermute(block, "core", [(0, 1), (1, 0)])


def flip(block, mask, chips):
    return lax.ppermute(block, CHIPS, [(i, i ^ mask) for i in range(chips)])


def sum_chips(block, chips, fans):
    mask = 1
    for most in fans + fans[-1:] * chips:
        if mask == chips:
            break
        fan = min(most, chips // mask)
        others = [flip(block, k * mask, chips) for k in range(1, fan)]
        if fan == 4:
            block = (block + others[0]) + (others[1] + others[2])
        else:
            block = block + others[0]
        mask *= fan
    return block


def exchange(blocks):
    return lax.all_to_all(blocks, CHIPS, split_axis=0, concat_axis=0, tiled=True)


def step(
    flow_state,
    diffusion,
    wall_stress,
    batch_counts,
    batch_routes,
    wall_index,
    input_weight,
    middle_weight,
    output_weight,
):
    tile_count, capacity = wall_index.shape
    chips = lax.axis_size(CHIPS)
    devices = chips * CORES
    assert chips & (chips - 1) == 0
    chip, core = lax.axis_index(CHIPS), lax.axis_index("core")
    rows_dev, hidden = middle_weight.shape
    width = hidden // chips
    live_dev = 5 * tile_count * capacity // 8
    lanes = LANE
    while lanes < live_dev:
        lanes *= 2
    group = max(1, min(chips, TILE // lanes))
    scale = grad_number / math.sqrt(live_dev * devices)

    order = [(i, (i + 1) % devices) for i in range(devices)]
    back_order = [(b, a) for a, b in order]
    place = jnp.stack([core, chip]).astype(jnp.int32)
    joint = lanes == width and rows_dev % ROWS == 0
    far = lambda array: pltpu.with_memory_space_constraint(array, pltpu.HBM)
    own, info, *blocks = pick_samples(
        far(batch_counts),
        far(batch_routes.reshape(1, tile_count)),
        far(wall_index.T),
        far(flow_state),
        far(middle_weight),
        lanes,
        (chips, rows_dev + ROWS, width) if joint else None,
    )
    blocks = [pltpu.with_memory_space_constraint(b, pltpu.VMEM) for b in blocks]
    first_z, last_z = edge_planes(flow_state)
    below = lax.ppermute(last_z, EVERY, order)
    above = lax.ppermute(first_z, EVERY, back_order)
    if joint:
        mine = exchange(blocks[0])
        got, skip = mine, rows_dev // ROWS
    else:
        mine = exchange(
            jnp.transpose(middle_weight.reshape(rows_dev, chips, width), (1, 0, 2))
        )
        got, skip = None, 0
    if not joint:
        got = exchange(jnp.broadcast_to(own, (chips, ROWS, lanes)))
    other = pltpu.with_memory_space_constraint(swap_cores(mine), pltpu.VMEM)

    win = widen(input_weight)
    wout = lax.dynamic_slice_in_dim(output_weight, chip * width, width, axis=1)
    keep = chips * lanes * hidden * 2 <= KEEP_BYTES
    if keep:
        rows, *first = first_layer(got, skip, win, group)
        second, part, weight = second_layer(
            place, first[0], mine, other, wout, rows_dev, group * lanes
        )
    else:
        first = []
        second, part, rows, weight = forward(
            place, got, skip, mine, other, win, wout, rows_dev, group
        )
    pred = sum_chips(part, chips, (4,))

    stay, send = middle_gradient(
        place, rows, win, wout, second, pred, first, rows_dev, group, live_dev, scale
    )
    summed = stay + swap_cores(send)
    grad = exchange(summed)
    grad_w_mid = lay_rows(grad)

    stay, send = input_gradient(
        place, rows, win, wout, weight, second, pred, own, info, group, live_dev, scale, devices
    )
    half = stay + swap_cores(send)
    half = sum_chips(half, chips, (4, 2))
    rest = swap_cores(half)
    grad_w_in, loss = join_halves(place, half, rest)
    batch_loss = loss.reshape(1)

    field = slab(flow_state, diffusion)
    new_stress, field = wall(place, info, pred, wall_stress, field)
    new_field = rim(below, above, far(diffusion), field)
    return (new_field, new_stress, batch_loss, grad_w_in, grad_w_mid)


def solution(mesh):
    sec, dev = mesh.shape["sec"], mesh.shape["dev"]
    inner = Mesh(mesh.devices.reshape(sec, dev // CORES, CORES), EVERY)
    in_specs = (
        P(None, None, EVERY, None),
        P(None, EVERY, None),
        P(None, EVERY, None),
        P(EVERY, None),
        P(EVERY, None),
        P(EVERY, None),
        P(),
        P(EVERY, None),
        P(),
    )
    out_specs = (
        P(None, None, EVERY, None),
        P(None, EVERY, None),
        P(EVERY),
        P(),
        P(EVERY, None),
    )
    return jax.shard_map(
        step, mesh=inner, in_specs=in_specs, out_specs=out_specs, check_vma=False
    )
```
